256 devices in a mesh: member: 8 (over x, core), lat: 32 (over z, y).
Axes of the slice: x: 4, y: 4, z: 8, core: 2. Of those that a mesh axis runs over, the one named last changes fastest.
Arguments:
- velocity: bfloat16 [16, 8, 1024, 2048], P('member', None, 'lat'), may hold values from -6 to 6
- tracer: bfloat16 [16, 8, 1024, 2048], P('member', None, 'lat'), may hold values from -6 to 6
- wave_slots: int32 [768], replicated, may hold values from 0 to 767, each once
- parents: int32 [16], replicated, may hold values from 0 to 15, as said below
- noise: bfloat16 [768, 16, 2, 8, 683], P('lat', 'member'), may hold values from -4 to 4
Outputs:
- child_spectra: bfloat16 [768, 16, 2, 8, 683], P('lat', 'member')
- child_fourier: bfloat16 [768, 16, 2, 8, 1024], P('lat', 'member')
The draws below stay inside these ranges and needn't reach their ends.
Inputs may be any that keep to these rules, and one draw needn't show every extreme that they name: `wave_slots`: each number below 683 stands in exactly one slot; a slot holding 683 or more is empty. `parents`: the parent of child i lies within 2 of i, and some child's parent is exactly 2 above it.
All inputs are finite; a program needn't handle non-finite values.
Results may differ from the reference program's by a relative error of at most 0.008.
Values may be sent and summed in bfloat16 or wider, within the bound.
A program may use at most 64 MiB of HBM per device.

```python
import math
import jax
import jax.numpy as jnp
from jax import lax

NLAT = 1024
NLON = 2048
TRUNC = 683
FIELDS = 8
SPREAD = 2
MEM_DEV = 2
MEMBERS = 16
MPAD = 768


def draw_parents(key, part):
    index = jnp.arange(MEMBERS, dtype=jnp.int32)
    position = index % MEM_DEV
    offsets = jax.random.randint(jax.random.fold_in(key, 11), (MEMBERS,), -SPREAD, SPREAD + 1)
    below = jax.random.randint(jax.random.fold_in(key, 12), (MEMBERS,), -SPREAD, 0)
    above = jax.random.randint(jax.random.fold_in(key, 13), (MEMBERS,), 1, SPREAD + 1)
    first_child = (position == 0) & (index >= MEM_DEV)
    last_child = (position == MEM_DEV - 1) & (index < MEMBERS - MEM_DEV)
    offsets = jnp.where(first_child, below, offsets)
    offsets = jnp.where(last_child, above, offsets)
    offsets = jnp.where(index == MEM_DEV - 1, SPREAD, offsets)
    return jnp.clip(index + offsets, 0, MEMBERS - 1).astype(jnp.int32)


def steps_of(key, shape, shards, least, top_value):
    factor_of = 1.0
    for axis_at, parts in shards:
        draws = jax.random.uniform(jax.random.fold_in(jax.random.fold_in(key, 6), axis_at), (parts,), jnp.float32, least / len(shards), top_value / len(shards))
        factor_of = factor_of * jnp.repeat(jnp.exp(draws), shape[axis_at] // parts).reshape((-1,) + (1,) * (len(shape) - 1 - axis_at))
    return factor_of


def normal_values(key, shape, scale, bound, cuts=(), held_as=jnp.bfloat16):
    values = jax.random.normal(key, shape, jnp.float32) * scale
    if len(cuts) > 0:
        values = steps_of(key, shape, cuts, -0.22, 0.18) * values
    return jnp.clip(values, min=-bound, max=bound).astype(held_as)


def setup_inputs(seed: int = 0) -> dict:
    key_list = jax.random.split(jax.random.key(seed), 6)
    return {
        "velocity": normal_values(key_list[0], (MEMBERS, FIELDS, NLAT, NLON), 1.0, 6.0, ((0, 8), (2, 32))),
        "tracer": normal_values(key_list[1], (MEMBERS, FIELDS, NLAT, NLON), 1.0, 6.0, ((0, 8), (2, 32))),
        "wave_slots": jax.random.permutation(key_list[2], MPAD).astype(jnp.int32),
        "parents": draw_parents(jax.random.fold_in(key_list[5], 71), 0),
        "noise": normal_values(key_list[4], (MPAD, MEMBERS, 2, FIELDS, TRUNC), 0.5, 4.0, ((0, 32), (1, 8))),
    }


def zonal_table(wavenumbers):
    longitude = jnp.arange(NLON, dtype=jnp.int32)
    active = (wavenumbers < TRUNC).astype(jnp.float32)
    phase = wavenumbers[:, None] * longitude[None, :] % NLON
    angle = phase.astype(jnp.float32) * (2.0 * math.pi / NLON)
    weight = active[:, None] / math.sqrt(NLON)
    table = jnp.stack([jnp.cos(angle) * weight, -jnp.sin(angle) * weight], axis=1)
    return table.astype(jnp.bfloat16)

def meridional_table(wavenumbers):
    degree = jnp.arange(TRUNC, dtype=jnp.int32)
    latitude = jnp.arange(NLAT, dtype=jnp.int32)
    phase = degree[:, None] * (2 * latitude + 1)[None, :] % (4 * NLAT)
    angle = phase.astype(jnp.float32) * (math.pi / (2 * NLAT))
    factor = math.sqrt(2.0 / NLAT)
    even_table = (jnp.cos(angle) * factor).astype(jnp.bfloat16)
    odd_table = (jnp.sin(angle) * factor).astype(jnp.bfloat16)
    active = (degree[None, :] >= wavenumbers[:, None]) & (wavenumbers[:, None] < TRUNC)
    is_odd = (wavenumbers % 2 == 1)[:, None, None]
    table = jnp.where(is_odd, odd_table[None], even_table[None])
    return jnp.where(active[:, :, None], table, jnp.zeros((), jnp.bfloat16))

def reference(velocity, tracer, wave_slots, parents, noise):
    members = velocity.shape[0]
    product = (velocity.astype(jnp.float32) * tracer.astype(jnp.float32)).astype(jnp.bfloat16)
    table = zonal_table(wave_slots).reshape(-1, NLON)
    flat = product.reshape(-1, NLON)
    fourier = lax.dot_general(table, flat, (((1,), (1,)), ((), ())), preferred_element_type=jnp.float32)
    fourier = fourier.astype(jnp.bfloat16).reshape(MPAD, 2, members, FIELDS, NLAT)
    fourier = jnp.transpose(fourier, (0, 2, 1, 3, 4))
    degree = jnp.arange(TRUNC, dtype=jnp.int32)

    def per_slot(entries):
        wavenumber, coefficients, perturbation = entries
        basis = meridional_table(wavenumber[None])[0]
        spectra = jnp.dot(coefficients.reshape(-1, NLAT), basis.T, preferred_element_type=jnp.float32)
        spectra = spectra.astype(jnp.bfloat16).reshape(members, 2, FIELDS, TRUNC)
        parent_rows = spectra[parents]
        active = ((degree >= wavenumber) & (wavenumber < TRUNC)).astype(jnp.float32)
        children = (parent_rows.astype(jnp.float32) + perturbation.astype(jnp.float32) * active).astype(jnp.bfloat16)
        returned = jnp.dot(children.reshape(-1, TRUNC), basis, preferred_element_type=jnp.float32)
        return (children, returned.astype(jnp.bfloat16).reshape(members, 2, FIELDS, NLAT))
    child_spectra, child_fourier = lax.map(per_slot, (wave_slots, fourier, noise))
    return (child_spectra, child_fourier)
```

```python
import functools
import math

import jax
import jax.numpy as jnp
from jax import lax
from jax.experimental import pallas as pl
from jax.experimental.pallas import tpu as pltpu
from jax.sharding import PartitionSpec as P

NLAT = 1024
NLON = 2048
TRUNC = 683
NPAD = 768
SPREAD = 2
SG = 8
MESH = pl.DeviceIdType.MESH
F32 = jnp.float32
BF16 = jnp.bfloat16
NT = (((1,), (1,)), ((), ()))
NN = (((1,), (0,)), ((), ()))


def iota(shape, dim):
    return lax.broadcasted_iota(jnp.int32, shape, dim)


def cos_sin(phase, period):
    eighth = period // 8
    quarter = period // 4
    shifted = phase + eighth
    quad = (shifted // quarter) & 3
    x = ((shifted & (quarter - 1)) - eighth).astype(F32) * (2.0 * math.pi / period)
    y = x * x
    s = x * (1.0 + y * (-1.0 / 6 + y * (1.0 / 120 + y * (-1.0 / 5040 + y * (1.0 / 362880)))))
    c = 1.0 + y * (-0.5 + y * (1.0 / 24 + y * (-1.0 / 720 + y * (1.0 / 40320))))
    odd = (quad & 1) == 1
    cos = jnp.where(odd, s, c)
    sin = jnp.where(odd, c, s)
    cos = jnp.where((quad == 1) | (quad == 2), -cos, cos)
    sin = jnp.where(quad >= 2, -sin, sin)
    return cos, sin


def kernel(
    lat_count, member_count,
    parents, waves, waves_row, velocity, tracer, noise,
    spectra_out, fourier_out,
    wave_b, vel, tra, prod, table, four, low, high, sel, recv, even_t, odd_t,
    xmat, spec, kids, noise_v, spec_v, four_v,
    in_sem, noise_sem, xs_sem, xr_sem, as_sem, ar_sem, out_sem,
):
    me = lax.axis_index("lat")
    group = lax.axis_index("member")
    chunks = four.shape[0]
    slots_here = chunks * SG
    lat_local = NLAT // lat_count
    mf = vel.shape[0] // lat_local
    fields = mf // 2

    barrier = pltpu.get_barrier_semaphore()
    up = lax.rem(group + 1, member_count)
    down = lax.rem(group + member_count - 1, member_count)

    load_v = pltpu.make_async_copy(velocity, vel, in_sem.at[0])
    load_t = pltpu.make_async_copy(tracer, tra, in_sem.at[1])
    load_v.start()
    load_t.start()

    @pl.loop(1, lat_count)
    def _(o):
        pl.semaphore_signal(
            barrier, inc=1, device_id={"lat": lax.rem(me + o, lat_count)}, device_id_type=MESH
        )

    pl.semaphore_signal(barrier, inc=1, device_id={"member": up}, device_id_type=MESH)
    pl.semaphore_signal(barrier, inc=1, device_id={"member": down}, device_id_type=MESH)
    load_n = pltpu.make_async_copy(noise, noise_v, noise_sem)
    load_n.start()

    for r in range(waves_row.shape[0]):
        row = waves_row[r : r + 1, :].astype(F32)
        wave_b[128 * r : 128 * r + 128, :] = jnp.transpose(jnp.broadcast_to(row, (128, 128)))

    def make_table(q):
        @pl.loop(0, lat_count)
        def _(d):
            w = wave_b[pl.ds(pl.multiple_of(d * slots_here + q * SG, SG), SG), :].astype(jnp.int32)
            c, s = cos_sin((w * iota((SG, 128), 1)) & (NLON - 1), NLON)
            ct, st = cos_sin((w * 128) & (NLON - 1), NLON)
            weight = jnp.where(w < TRUNC, 1.0 / math.sqrt(NLON), 0.0)
            c = c * weight
            s = -s * weight
            sign = jnp.where((w & 1) == 1, -1.0, 1.0)
            rows = pl.ds(pl.multiple_of(d * 2 * SG, 2 * SG), 2 * SG)
            half = NLON // 2
            for t in range(half // 128):
                here = jnp.concatenate([c, s], axis=0)
                there = jnp.concatenate([c * sign, s * sign], axis=0)
                table[rows, 128 * t : 128 * t + 128] = here.astype(BF16)
                table[rows, half + 128 * t : half + 128 * t + 128] = there.astype(BF16)
                if t + 1 < half // 128:
                    c, s = c * ct + s * st, s * ct - c * st

    def zonal(q):
        make_table(q)
        per = 16

        @pl.loop(0, lat_count // per)
        def _(b):
            rows = pl.ds(pl.multiple_of(b * per * 2 * SG, per * 2 * SG), per * 2 * SG)
            out = lax.dot_general(table[rows, :], prod[...], NT, preferred_element_type=F32)
            four[q, pl.ds(b * per, per)] = out.astype(BF16).reshape(per, 2 * SG, out.shape[1])

    load_v.wait()
    load_t.wait()

    @pl.loop(0, vel.shape[0] // 16)
    def _(b):
        rows = pl.ds(pl.multiple_of(b * 16, 16), 16)
        prod[rows, :] = (vel[rows, :].astype(F32) * tra[rows, :].astype(F32)).astype(BF16)

    def x_copies(q):
        to_up = pltpu.make_async_remote_copy(
            src_ref=four.at[q], dst_ref=low.at[q], send_sem=xs_sem.at[q, 0], recv_sem=xr_sem.at[q, 0],
            device_id={"member": up}, device_id_type=MESH,
        )
        to_down = pltpu.make_async_remote_copy(
            src_ref=four.at[q], dst_ref=high.at[q], send_sem=xs_sem.at[q, 1], recv_sem=xr_sem.at[q, 1],
            device_id={"member": down}, device_id_type=MESH,
        )
        return to_up, to_down

    def a_copy(q, target):
        return pltpu.make_async_remote_copy(
            src_ref=sel.at[q, target], dst_ref=recv.at[q, me],
            send_sem=as_sem.at[q], recv_sem=ar_sem.at[q],
            device_id={"lat": target}, device_id_type=MESH,
        )

    zonal(0)
    pl.semaphore_wait(barrier, lat_count + 1)
    for c in x_copies(0):
        c.start()
    for q in range(1, chunks):
        zonal(q)
        for c in x_copies(q):
            c.start()

    def make_basis():
        step = 64
        half_turn = 2 * NLAT
        lanes = 128

        @pl.loop(0, NLAT // lanes)
        def _(jt):
            j = jt * lanes + iota((8, lanes), 1)
            sub = iota((8, lanes), 0)
            c8, s8 = cos_sin((8 * (2 * j + 1)) & (2 * half_turn - 1), 2 * half_turn)
            cols = pl.ds(pl.multiple_of(jt * lanes, lanes), lanes)
            scale = math.sqrt(2.0 / NLAT)

            @pl.loop(0, NPAD // step)
            def _(a):
                n = a * step + sub
                c, s = cos_sin((n * (2 * j + 1)) & (2 * half_turn - 1), 2 * half_turn)
                c = c * scale
                s = s * scale
                for b in range(step // 16):
                    c2, s2 = c * c8 - s * s8, s * c8 + c * s8
                    n16 = pl.ds(pl.multiple_of(a * step + b * 16, 16), 16)
                    even_t[n16, cols] = jnp.concatenate([c, c2], axis=0).astype(BF16)
                    odd_t[n16, cols] = jnp.concatenate([s, s2], axis=0).astype(BF16)
                    c, s = c2 * c8 - s2 * s8, s2 * c8 + c2 * s8

    make_basis()

    first = group * 2
    for q in range(chunks):
        for c in x_copies(q):
            c.wait_recv()
        halves = mf // 2 * lat_local
        for m in range(2):
            place = parents[first + m] - first + SPREAD

            @pl.loop(0, lat_count)
            def _(d):
                chosen = None
                for p in range(m, m + 2 * SPREAD + 1):
                    source = (low, four, high)[p // 2]
                    cand = source[q, d, :, (p % 2) * halves : (p % 2 + 1) * halves]
                    hit = jnp.broadcast_to(place == p, cand.shape)
                    chosen = cand if chosen is None else jnp.where(hit, cand, chosen)
                sel[q, d, :, m * halves : (m + 1) * halves] = chosen

        @pl.loop(1, lat_count)
        def _(o):
            a_copy(q, lax.rem(me + o, lat_count)).start()

        recv[q, me] = sel[q, me]

    load_n.wait()
    kids[...] = jnp.zeros_like(kids)

    for q in range(chunks):
        pltpu.make_async_remote_copy(
            src_ref=recv.at[q, pl.ds(0, lat_count - 1)], dst_ref=recv.at[q, pl.ds(0, lat_count - 1)],
            send_sem=as_sem.at[q], recv_sem=ar_sem.at[q], device_id={"lat": me}, device_id_type=MESH,
        ).wait_recv()
        lane = iota((2 * SG, 128), 1)
        per = 128 // lat_local
        for t in range(mf // per):
            @pl.loop(0, lat_count // per)
            def _(p):
                cols = slice(128 * t, 128 * t + 128)
                parts = [recv[q, p * per + i, :, cols] for i in range(per)]
                for k in range(per):
                    xmat[pl.ds((t * per + k) * 2 * SG, 2 * SG), pl.ds(pl.multiple_of(p * 128, 128), 128)] = (
                        jnp.concatenate([a[:, k * lat_local : (k + 1) * lat_local] for a in parts], axis=1)
                    )
        w = wave_b[pl.ds(pl.multiple_of(me * slots_here + q * SG, SG), SG), :].astype(jnp.int32)
        x = xmat[...]
        for nt in range(NPAD // 256):
            cols = slice(256 * nt, 256 * nt + 256)
            even = lax.dot_general(x, even_t[cols, :], NT, preferred_element_type=F32)
            odd = lax.dot_general(x, odd_t[cols, :], NT, preferred_element_type=F32)
            for half in range(2):
                n = 256 * nt + 128 * half + iota((SG, 128), 1)
                live = (n >= w) & (w < TRUNC) & (n < TRUNC)
                is_odd = (w & 1) == 1
                lanes = slice(128 * half, 128 * half + 128)
                for i in range(mf * 2):
                    member, field, part = i // (2 * fields), i // 2 % fields, i % 2
                    rows = slice(SG * i, SG * i + SG)
                    value = jnp.where(is_odd, odd[rows, lanes], even[rows, lanes])
                    value = jnp.where(live, value, 0.0)
                    start = member * 2 * fields + part * fields + field
                    start = start + (2 * nt + half) * SG * 2 * mf
                    spec[pl.ds(start, SG, stride=2 * mf), :] = value

        for s in range(SG):
            wave = waves[me * slots_here + q * SG + s]
            rows = slice(s * 2 * mf, (s + 1) * 2 * mf)
            out_rows = slice((q * SG + s) * 2 * mf, (q * SG + s + 1) * 2 * mf)
            n = iota((2 * mf, TRUNC), 1)
            live = (n >= wave) & (wave < TRUNC)
            base = jnp.concatenate(
                [spec[pl.ds((t * SG + s) * 2 * mf, 2 * mf), :] for t in range(NPAD // 128)], axis=1
            )[:, :TRUNC].astype(BF16).astype(F32)
            extra = noise_v[out_rows, :].astype(F32)
            child = (base + jnp.where(live, extra, 0.0)).astype(BF16)
            spec_v[out_rows, :] = child
            kids[rows, :TRUNC] = child

        for nt in range(NLAT // 256):
            cols = slice(256 * nt, 256 * nt + 256)
            even = lax.dot_general(kids[...], even_t[:, cols], NN, preferred_element_type=F32)
            odd = lax.dot_general(kids[...], odd_t[:, cols], NN, preferred_element_type=F32)
            for s in range(SG):
                wave = waves[me * slots_here + q * SG + s]
                rows = slice(s * 2 * mf, (s + 1) * 2 * mf)
                is_odd = jnp.broadcast_to((wave & 1) == 1, (2 * mf, 256))
                value = jnp.where(is_odd, odd[rows], even[rows])
                four_v[q * SG * 2 * mf + s * 2 * mf : q * SG * 2 * mf + (s + 1) * 2 * mf, cols] = value.astype(BF16)

        block = pl.ds(q * SG * 2 * mf, SG * 2 * mf)
        pltpu.make_async_copy(spec_v.at[block], spectra_out.at[block], out_sem.at[q, 0]).start()
        pltpu.make_async_copy(four_v.at[block], fourier_out.at[block], out_sem.at[q, 1]).start()

    for q in range(chunks):
        for c in x_copies(q):
            c.wait_send()
        pltpu.make_async_remote_copy(
            src_ref=sel.at[q, pl.ds(0, lat_count - 1)], dst_ref=recv.at[q, pl.ds(0, lat_count - 1)],
            send_sem=as_sem.at[q], recv_sem=ar_sem.at[q], device_id={"lat": me}, device_id_type=MESH,
        ).wait_send()
        block = pl.ds(q * SG * 2 * mf, SG * 2 * mf)
        pltpu.make_async_copy(spec_v.at[block], spectra_out.at[block], out_sem.at[q, 0]).wait()
        pltpu.make_async_copy(four_v.at[block], fourier_out.at[block], out_sem.at[q, 1]).wait()


def per_device(lat_count, member_count, velocity, tracer, wave_slots, parents, noise):
    mem, fields, lat_local, lon = velocity.shape
    slots = wave_slots.shape[0]
    here = slots // lat_count
    chunks = here // SG
    rows = mem * fields * lat_local
    mf = mem * fields
    out_rows = here * mem * 2 * fields
    chunk_rows = SG * 2 * mf
    any_spec = pl.BlockSpec(memory_space=pl.ANY)
    smem = pl.BlockSpec(memory_space=pltpu.SMEM)
    vmem = pl.BlockSpec(memory_space=pltpu.VMEM)
    msg = (chunks, lat_count, 2 * SG, rows)
    dma = pltpu.SemaphoreType.DMA
    spectra, fourier = pl.pallas_call(
        functools.partial(kernel, lat_count, member_count),
        out_shape=(
            jax.ShapeDtypeStruct((out_rows, TRUNC), BF16),
            jax.ShapeDtypeStruct((out_rows, NLAT), BF16),
        ),
        in_specs=[smem, smem, vmem, any_spec, any_spec, any_spec],
        out_specs=(any_spec, any_spec),
        scratch_shapes=[
            pltpu.VMEM((slots, 128), F32),
            pltpu.VMEM((rows, lon), BF16),
            pltpu.VMEM((rows, lon), BF16),
            pltpu.VMEM((rows, lon), BF16),
            pltpu.VMEM((lat_count * 2 * SG, lon), BF16),
            pltpu.VMEM(msg, BF16),
            pltpu.VMEM(msg, BF16),
            pltpu.VMEM(msg, BF16),
            pltpu.VMEM(msg, BF16),
            pltpu.VMEM(msg, BF16),
            pltpu.VMEM((NPAD, NLAT), BF16),
            pltpu.VMEM((NPAD, NLAT), BF16),
            pltpu.VMEM((chunk_rows, NLAT), BF16),
            pltpu.VMEM((NPAD // 128 * chunk_rows, 128), F32),
            pltpu.VMEM((chunk_rows, NPAD), BF16),
            pltpu.VMEM((out_rows, TRUNC), BF16),
            pltpu.VMEM((out_rows, TRUNC), BF16),
            pltpu.VMEM((out_rows, NLAT), BF16),
            dma((2,)),
            dma,
            dma((chunks, 2)),
            dma((chunks, 2)),
            dma((chunks,)),
            dma((chunks,)),
            dma((chunks, 2)),
        ],
        compiler_params=pltpu.CompilerParams(
            collective_id=0, has_side_effects=True, vmem_limit_bytes=60 * 1024 * 1024
        ),
        name="transform",
    )(
        parents,
        wave_slots,
        wave_slots.reshape(slots // 128, 128),
        velocity.reshape(rows, lon),
        tracer.reshape(rows, lon),
        noise.reshape(out_rows, TRUNC),
    )
    return (
        spectra.reshape(here, mem, 2, fields, TRUNC),
        fourier.reshape(here, mem, 2, fields, NLAT),
    )


def solution(mesh):
    in_specs = (
        P("member", None, "lat", None),
        P("member", None, "lat", None),
        P(),
        P(),
        P("lat", "member", None, None, None),
    )
    out_specs = (P("lat", "member", None, None, None), P("lat", "member", None, None, None))
    return jax.shard_map(
        functools.partial(per_device, mesh.shape["lat"], mesh.shape["member"]),
        mesh=mesh, in_specs=in_specs, out_specs=out_specs, check_vma=False,
    )
```

```python
import functools
import math

import jax
import jax.numpy as jnp
from jax import lax
from jax.experimental import pallas as pl
from jax.experimental.pallas import tpu as pltpu
from jax.sharding import PartitionSpec as P

NLAT = 1024
NLON = 2048
TRUNC = 683
NPAD = 768
SPREAD = 2
SG = 8
MESH = pl.DeviceIdType.MESH
F32 = jnp.float32
BF16 = jnp.bfloat16
NT = (((1,), (1,)), ((), ()))
NN = (((1,), (0,)), ((), ()))


def iota(shape, dim):
    return lax.broadcasted_iota(jnp.int32, shape, dim)


def cos_sin(phase, period):
    eighth = period // 8
    quarter = period // 4
    shifted = phase + eighth
    quad = (shifted // quarter) & 3
    x = ((shifted & (quarter - 1)) - eighth).astype(F32) * (2.0 * math.pi / period)
    y = x * x
    s = x * (1.0 + y * (-1.0 / 6 + y * (1.0 / 120 + y * (-1.0 / 5040 + y * (1.0 / 362880)))))
    c = 1.0 + y * (-0.5 + y * (1.0 / 24 + y * (-1.0 / 720 + y * (1.0 / 40320))))
    odd = (quad & 1) == 1
    cos = jnp.where(odd, s, c)
    sin = jnp.where(odd, c, s)
    cos = jnp.where((quad == 1) | (quad == 2), -cos, cos)
    sin = jnp.where(quad >= 2, -sin, sin)
    return cos, sin


def kernel(
    lat_count, member_count,
    parents_hbm, waves_hbm, waves_row_hbm, velocity, tracer, noise,
    spectra_out, fourier_out,
    parents, waves, waves_row, wave_b, vel, tra, prod, table, four, low, high, sel, recv, even_t, odd_t,
    xmat, spec, kids, noise_v, spec_v, four_v, own_s, low_s, high_s,
    small_sem, ss_sem, sr_sem, in_sem, noise_sem, xs_sem, xr_sem, as_sem, ar_sem, out_sem,
):
    me = lax.axis_index("lat")
    group = lax.axis_index("member")
    chunks = four.shape[0]
    slots_here = chunks * SG
    halves = 2
    half_count = lat_count // halves
    lat_local = NLAT // lat_count
    mf = vel.shape[0] // lat_local
    fields = mf // 2

    barrier = pltpu.get_barrier_semaphore()
    up = lax.rem(group + 1, member_count)
    down = lax.rem(group + member_count - 1, member_count)

    @pl.loop(1, lat_count)
    def _(o):
        pl.semaphore_signal(
            barrier, inc=1, device_id={"lat": lax.rem(me + o, lat_count)}, device_id_type=MESH
        )

    pl.semaphore_signal(barrier, inc=1, device_id={"member": up}, device_id_type=MESH)
    pl.semaphore_signal(barrier, inc=1, device_id={"member": down}, device_id_type=MESH)
    load_w = pltpu.make_async_copy(waves_row_hbm, waves_row, small_sem.at[0])
    load_w.start()
    load_v = pltpu.make_async_copy(velocity, vel, in_sem.at[0])
    load_t = pltpu.make_async_copy(tracer, tra, in_sem.at[1])
    load_v.start()
    load_t.start()
    load_s = pltpu.make_async_copy(waves_hbm, waves, small_sem.at[1])
    load_s.start()
    load_p = pltpu.make_async_copy(parents_hbm, parents, small_sem.at[2])
    load_p.start()
    load_n = pltpu.make_async_copy(noise, noise_v, noise_sem)
    load_n.start()
    load_w.wait()

    for r in range(waves_row.shape[0]):
        row = waves_row[r : r + 1, :].astype(F32)
        wave_b[128 * r : 128 * r + 128, :] = jnp.transpose(jnp.broadcast_to(row, (128, 128)))

    y_count = 128 // lat_local
    z_count = lat_count // y_count
    my_z, my_y = me // y_count, lax.rem(me, y_count)

    def turn_of(k):
        r = z_count - 1 - k
        return (r + 1) // 2 * (1 - 2 * lax.rem(r + 1, 2))

    def target_of(i):
        z = lax.rem(my_z + turn_of(i // y_count) + z_count, z_count)
        return z * y_count + lax.rem(my_y + i + 1, y_count)

    def make_table(q, first):
        together = 4

        @pl.loop(0, half_count // together)
        def _(b):
            w = jnp.concatenate(
                [
                    wave_b[
                        pl.ds(pl.multiple_of(target_of(first + b * together + j) * slots_here + q * SG, SG), SG), :
                    ]
                    for j in range(together)
                ],
                axis=0,
            ).astype(jnp.int32)
            c, s = cos_sin((w * iota(w.shape, 1)) & (NLON - 1), NLON)
            ct, st = cos_sin((w * 128) & (NLON - 1), NLON)
            weight = jnp.where(w < TRUNC, 1.0 / math.sqrt(NLON), 0.0)
            c = c * weight
            s = -s * weight
            sign = jnp.where((w & 1) == 1, -1.0, 1.0)
            half = NLON // 2
            for t in range(half // 128):
                for factor, offset in ((None, 0), (sign, half)):
                    cc = c if factor is None else c * factor
                    ss = s if factor is None else s * factor
                    for j in range(together):
                        part = slice(j * SG, j * SG + SG)
                        rows = pl.ds(pl.multiple_of((b * together + j) * 2 * SG, 2 * SG), 2 * SG)
                        table[rows, offset + 128 * t : offset + 128 * t + 128] = jnp.concatenate(
                            [cc[part], ss[part]], axis=0
                        ).astype(BF16)
                if t + 1 < half // 128:
                    c, s = c * ct + s * st, s * ct - c * st

    def zonal(q, h):
        first = h * half_count
        make_table(q, first)
        out = lax.dot_general(table[...], prod[...], NT, preferred_element_type=F32)
        four[q, first : first + half_count] = out.astype(BF16).reshape(half_count, 2 * SG, out.shape[1])

    load_v.wait()
    load_t.wait()

    @pl.loop(0, vel.shape[0] // 16)
    def _(b):
        rows = pl.ds(pl.multiple_of(b * 16, 16), 16)
        prod[rows, :] = (vel[rows, :].astype(F32) * tra[rows, :].astype(F32)).astype(BF16)

    def x_copies(q, h):
        block = pl.ds(h * half_count, half_count)
        to_up = pltpu.make_async_remote_copy(
            src_ref=four.at[q, block], dst_ref=low.at[q, block],
            send_sem=xs_sem.at[q, h, 0], recv_sem=xr_sem.at[q, h, 0],
            device_id={"member": up}, device_id_type=MESH,
        )
        to_down = pltpu.make_async_remote_copy(
            src_ref=four.at[q, block], dst_ref=high.at[q, block],
            send_sem=xs_sem.at[q, h, 1], recv_sem=xr_sem.at[q, h, 1],
            device_id={"member": down}, device_id_type=MESH,
        )
        return to_up, to_down

    def send_half(q, h, source):
        first = h * half_count
        last = h == halves - 1

        @pl.loop(first, first + half_count - (1 if last else 0))
        def _(i):
            pltpu.make_async_remote_copy(
                src_ref=source.at[q, i], dst_ref=recv.at[q, me],
                send_sem=as_sem.at[q], recv_sem=ar_sem.at[q, my_z],
                device_id={"lat": target_of(i)}, device_id_type=MESH,
            ).start()

        if last:
            recv[q, me] = source[q, lat_count - 1]

    zonal(0, 0)
    pl.semaphore_wait(barrier, lat_count + 1)
    send_half(0, 0, four)
    zonal(0, 1)
    send_half(0, 1, four)
    for q in range(1, chunks):
        for h in range(halves):
            zonal(q, h)
            for c in x_copies(q, h):
                c.start()

    def make_basis():
        step = 64
        half_turn = 2 * NLAT
        lanes = 128

        @pl.loop(0, NLAT // lanes)
        def _(jt):
            j = jt * lanes + iota((8, lanes), 1)
            sub = iota((8, lanes), 0)
            c8, s8 = cos_sin((8 * (2 * j + 1)) & (2 * half_turn - 1), 2 * half_turn)
            cols = pl.ds(pl.multiple_of(jt * lanes, lanes), lanes)
            scale = math.sqrt(2.0 / NLAT)

            @pl.loop(0, NPAD // step)
            def _(a):
                n = a * step + sub
                c, s = cos_sin((n * (2 * j + 1)) & (2 * half_turn - 1), 2 * half_turn)
                c = c * scale
                s = s * scale
                for b in range(step // 16):
                    c2, s2 = c * c8 - s * s8, s * c8 + c * s8
                    n16 = pl.ds(pl.multiple_of(a * step + b * 16, 16), 16)
                    even_t[n16, cols] = jnp.concatenate([c, c2], axis=0).astype(BF16)
                    odd_t[n16, cols] = jnp.concatenate([s, s2], axis=0).astype(BF16)
                    c, s = c2 * c8 - s2 * s8, s2 * c8 + c2 * s8

    load_s.wait()
    load_p.wait()
    first_member = group * 2
    places = [parents[first_member + m] - first_member + SPREAD for m in range(2)]

    def select_half(q, h):
        width = fields * lat_local

        @pl.loop(h * half_count, (h + 1) * half_count)
        def _(i):
            for m in range(2):
                chosen = None
                for p in range(m, m + 2 * SPREAD + 1):
                    source = (low, four, high)[p // 2]
                    cand = source[q, i, :, (p % 2) * width : (p % 2 + 1) * width]
                    hit = jnp.broadcast_to(places[m] == p, cand.shape)
                    chosen = cand if chosen is None else jnp.where(hit, cand, chosen)
                sel[q, i, :, m * width : (m + 1) * width] = chosen

    def relay(q, h):
        for c in x_copies(q, h):
            c.wait_recv()
        select_half(q, h)
        send_half(q, h, sel)

    for q in range(1, chunks):
        for h in range(halves):
            relay(q, h)

    make_basis()
    load_n.wait()
    kids[...] = jnp.zeros_like(kids)

    def arrive(q, p, count):
        block = recv.at[q, pl.ds(p * y_count, count)]
        pltpu.make_async_remote_copy(
            src_ref=block, dst_ref=block, send_sem=as_sem.at[q], recv_sem=ar_sem.at[q, p],
            device_id={"lat": me}, device_id_type=MESH,
        ).wait_recv()

    def shuffle(q):
        per = 128 // lat_local
        lane = iota((2 * SG, 128), 1) // lat_local
        low_half = lane < 2
        even_block = (lane & 1) == 0

        def swap(x, y, mask, width):
            left = jnp.where(mask, x, pltpu.roll(y, width, 1))
            right = jnp.where(mask, pltpu.roll(x, 128 - width, 1), y)
            return left, right

        def arrange(p):
            target = pl.ds(pl.multiple_of(p * 128, 128), 128)
            for t in range(mf // per):
                x0, x1, x2, x3 = [recv[q, p * per + i, :, 128 * t : 128 * t + 128] for i in range(per)]
                x0, x2 = swap(x0, x2, low_half, 2 * lat_local)
                x1, x3 = swap(x1, x3, low_half, 2 * lat_local)
                x0, x1 = swap(x0, x1, even_block, lat_local)
                x2, x3 = swap(x2, x3, even_block, lat_local)
                for k, x in enumerate((x0, x1, x2, x3)):
                    xmat[(t * per + k) * 2 * SG : (t * per + k + 1) * 2 * SG, target] = x

        @pl.loop(0, z_count - 1)
        def _(k):
            p = lax.rem(my_z - turn_of(k) + z_count, z_count)
            arrive(q, p, per)
            arrange(p)

        arrive(q, my_z, per - 1)
        arrange(my_z)

    def forward(q):
        shuffle(q)
        product(q)

    def product(q):
        w = wave_b[pl.ds(pl.multiple_of(me * slots_here + q * SG, SG), SG), :].astype(jnp.int32)
        x = xmat[...]
        for nt in range(NPAD // 256):
            cols = slice(256 * nt, 256 * nt + 256)
            even = lax.dot_general(x, even_t[cols, :], NT, preferred_element_type=F32)
            odd = lax.dot_general(x, odd_t[cols, :], NT, preferred_element_type=F32)
            for half in range(2):
                n = 256 * nt + 128 * half + iota((SG, 128), 1)
                live = (n >= w) & (w < TRUNC) & (n < TRUNC)
                is_odd = (w & 1) == 1
                lanes = slice(128 * half, 128 * half + 128)
                for i in range(mf * 2):
                    member, field, part = i // (2 * fields), i // 2 % fields, i % 2
                    rows = slice(SG * i, SG * i + SG)
                    value = jnp.where(is_odd, odd[rows, lanes], even[rows, lanes])
                    value = jnp.where(live, value, 0.0)
                    start = member * 2 * fields + part * fields + field
                    start = start + (2 * nt + half) * SG * 2 * mf
                    spec[pl.ds(start, SG, stride=2 * mf), :] = value

    def finish(q, base_of):
        for s in range(SG):
            wave = waves[me * slots_here + q * SG + s]
            rows = slice(s * 2 * mf, (s + 1) * 2 * mf)
            out_rows = slice((q * SG + s) * 2 * mf, (q * SG + s + 1) * 2 * mf)
            n = iota((2 * mf, TRUNC), 1)
            live = (n >= wave) & (wave < TRUNC)
            base = base_of(q, s).astype(F32)[:, :TRUNC]
            extra = noise_v[out_rows, :].astype(F32)
            child = (base + jnp.where(live, extra, 0.0)).astype(BF16)
            spec_v[out_rows, :] = child
            kids[rows, :TRUNC] = child

        for nt in range(NLAT // 256):
            cols = slice(256 * nt, 256 * nt + 256)
            even = lax.dot_general(kids[...], even_t[:, cols], NN, preferred_element_type=F32)
            odd = lax.dot_general(kids[...], odd_t[:, cols], NN, preferred_element_type=F32)
            for s in range(SG):
                wave = waves[me * slots_here + q * SG + s]
                rows = slice(s * 2 * mf, (s + 1) * 2 * mf)
                is_odd = jnp.broadcast_to((wave & 1) == 1, (2 * mf, 256))
                value = jnp.where(is_odd, odd[rows], even[rows])
                four_v[q * SG * 2 * mf + s * 2 * mf : q * SG * 2 * mf + (s + 1) * 2 * mf, cols] = value.astype(BF16)

        block = pl.ds(q * SG * 2 * mf, SG * 2 * mf)
        pltpu.make_async_copy(spec_v.at[block], spectra_out.at[block], out_sem.at[q, 0]).start()
        pltpu.make_async_copy(four_v.at[block], fourier_out.at[block], out_sem.at[q, 1]).start()

    def spec_of(q, s):
        tiles = [spec[pl.ds((t * SG + s) * 2 * mf, 2 * mf), :] for t in range(NPAD // 128)]
        return jnp.concatenate(tiles, axis=1).astype(BF16)

    def s_copies():
        to_up = pltpu.make_async_remote_copy(
            src_ref=own_s, dst_ref=low_s, send_sem=ss_sem.at[0], recv_sem=sr_sem.at[0],
            device_id={"member": up}, device_id_type=MESH,
        )
        to_down = pltpu.make_async_remote_copy(
            src_ref=own_s, dst_ref=high_s, send_sem=ss_sem.at[1], recv_sem=sr_sem.at[1],
            device_id={"member": down}, device_id_type=MESH,
        )
        return to_up, to_down

    def share():
        for s in range(SG):
            own_s[s * 2 * mf : (s + 1) * 2 * mf, :] = spec_of(0, s)
        for c in s_copies():
            c.start()

    def chosen_of(q, s):
        out = []
        for m in range(2):
            chosen = None
            for p in range(m, m + 2 * SPREAD + 1):
                source = (low_s, own_s, high_s)[p // 2]
                start = s * 2 * mf + (p % 2) * mf
                cand = source[start : start + mf, :]
                hit = jnp.broadcast_to(places[m] == p, cand.shape)
                chosen = cand if chosen is None else jnp.where(hit, cand, chosen)
            out.append(chosen)
        return jnp.concatenate(out, axis=0)

    forward(0)
    share()
    forward(1)
    finish(1, spec_of)
    for c in s_copies():
        c.wait_recv()
    finish(0, chosen_of)
    for q in range(2, chunks):
        forward(q)
        finish(q, spec_of)

    for c in s_copies():
        c.wait_send()
    for q in range(chunks):
        if q > 0:
            for h in range(halves):
                for c in x_copies(q, h):
                    c.wait_send()
        pltpu.make_async_remote_copy(
            src_ref=sel.at[q, pl.ds(0, lat_count - 1)], dst_ref=recv.at[q, pl.ds(0, lat_count - 1)],
            send_sem=as_sem.at[q], recv_sem=ar_sem.at[q, 0], device_id={"lat": me}, device_id_type=MESH,
        ).wait_send()
        block = pl.ds(q * SG * 2 * mf, SG * 2 * mf)
        pltpu.make_async_copy(spec_v.at[block], spectra_out.at[block], out_sem.at[q, 0]).wait()
        pltpu.make_async_copy(four_v.at[block], fourier_out.at[block], out_sem.at[q, 1]).wait()


def per_device(lat_count, member_count, velocity, tracer, wave_slots, parents, noise):
    mem, fields, lat_local, lon = velocity.shape
    slots = wave_slots.shape[0]
    here = slots // lat_count
    chunks = here // SG
    rows = mem * fields * lat_local
    mf = mem * fields
    out_rows = here * mem * 2 * fields
    chunk_rows = SG * 2 * mf
    any_spec = pl.BlockSpec(memory_space=pl.ANY)
    msg = (chunks, lat_count, 2 * SG, rows)
    dma = pltpu.SemaphoreType.DMA
    spectra, fourier = pl.pallas_call(
        functools.partial(kernel, lat_count, member_count),
        out_shape=(
            jax.ShapeDtypeStruct((out_rows, TRUNC), BF16),
            jax.ShapeDtypeStruct((out_rows, NLAT), BF16),
        ),
        in_specs=[any_spec] * 6,
        out_specs=(any_spec, any_spec),
        scratch_shapes=[
            pltpu.SMEM(parents.shape, jnp.int32),
            pltpu.SMEM((slots,), jnp.int32),
            pltpu.VMEM((slots // 128, 128), jnp.int32),
            pltpu.VMEM((slots, 128), F32),
            pltpu.VMEM((rows, lon), BF16),
            pltpu.VMEM((rows, lon), BF16),
            pltpu.VMEM((rows, lon), BF16),
            pltpu.VMEM((lat_count // 2 * 2 * SG, lon), BF16),
            pltpu.VMEM(msg, BF16),
            pltpu.VMEM(msg, BF16),
            pltpu.VMEM(msg, BF16),
            pltpu.VMEM(msg, BF16),
            pltpu.VMEM(msg, BF16),
            pltpu.VMEM((NPAD, NLAT), BF16),
            pltpu.VMEM((NPAD, NLAT), BF16),
            pltpu.VMEM((chunk_rows, NLAT), BF16),
            pltpu.VMEM((NPAD // 128 * chunk_rows, 128), F32),
            pltpu.VMEM((chunk_rows, NPAD), BF16),
            pltpu.VMEM((out_rows, TRUNC), BF16),
            pltpu.VMEM((out_rows, TRUNC), BF16),
            pltpu.VMEM((out_rows, NLAT), BF16),
            pltpu.VMEM((chunk_rows, NPAD), BF16),
            pltpu.VMEM((chunk_rows, NPAD), BF16),
            pltpu.VMEM((chunk_rows, NPAD), BF16),
            dma((3,)),
            dma((2,)),
            dma((2,)),
            dma((2,)),
            dma,
            dma((chunks, 2, 2)),
            dma((chunks, 2, 2)),
            dma((chunks,)),
            dma((chunks, lat_count * lat_local // 128)),
            dma((chunks, 2)),
        ],
        compiler_params=pltpu.CompilerParams(
            collective_id=0, has_side_effects=True, vmem_limit_bytes=60 * 1024 * 1024
        ),
        name="transform",
    )(
        parents,
        wave_slots,
        wave_slots.reshape(slots // 128, 128),
        velocity.reshape(rows, lon),
        tracer.reshape(rows, lon),
        noise.reshape(out_rows, TRUNC),
    )
    return (
        spectra.reshape(here, mem, 2, fields, TRUNC),
        fourier.reshape(here, mem, 2, fields, NLAT),
    )


def solution(mesh):
    in_specs = (
        P("member", None, "lat", None),
        P("member", None, "lat", None),
        P(),
        P(),
        P("lat", "member", None, None, None),
    )
    out_specs = (P("lat", "member", None, None, None), P("lat", "member", None, None, None))
    return jax.shard_map(
        functools.partial(per_device, mesh.shape["lat"], mesh.shape["member"]),
        mesh=mesh, in_specs=in_specs, out_specs=out_specs, check_vma=False,
    )
```

```python
import functools
import math

import jax
import jax.numpy as jnp
from jax import lax
from jax.experimental import pallas as pl
from jax.experimental.pallas import tpu as pltpu
from jax.sharding import PartitionSpec as P

NLAT = 1024
NLON = 2048
TRUNC = 683
NPAD = 768
SPREAD = 2
SG = 8
MESH = pl.DeviceIdType.MESH
F32 = jnp.float32
BF16 = jnp.bfloat16
NT = (((1,), (1,)), ((), ()))
NN = (((1,), (0,)), ((), ()))


def iota(shape, dim):
    return lax.broadcasted_iota(jnp.int32, shape, dim)


def cos_sin(phase, period):
    eighth = period // 8
    quarter = period // 4
    shifted = phase + eighth
    quad = (shifted // quarter) & 3
    x = ((shifted & (quarter - 1)) - eighth).astype(F32) * (2.0 * math.pi / period)
    y = x * x
    s = x * (1.0 + y * (-1.0 / 6 + y * (1.0 / 120 + y * (-1.0 / 5040 + y * (1.0 / 362880)))))
    c = 1.0 + y * (-0.5 + y * (1.0 / 24 + y * (-1.0 / 720 + y * (1.0 / 40320))))
    odd = (quad & 1) == 1
    cos = jnp.where(odd, s, c)
    sin = jnp.where(odd, c, s)
    cos = jnp.where((quad == 1) | (quad == 2), -cos, cos)
    sin = jnp.where(quad >= 2, -sin, sin)
    return cos, sin


def forward_rows(xmat, even_f, odd_f, wave, spec, mf):
    w = wave.astype(jnp.int32)
    fields = mf // 2
    is_odd = (w & 1) == 1
    x = xmat[...]
    for nt in range(NPAD // 256):
        cols = slice(256 * nt, 256 * nt + 256)
        even = lax.dot_general(x, even_f[:, cols], NN, preferred_element_type=F32)
        odd = lax.dot_general(x, odd_f[:, cols], NN, preferred_element_type=F32)
        for half in range(2):
            n = 256 * nt + 128 * half + iota((SG, 128), 1)
            live = (n >= w) & (w < TRUNC) & (n < TRUNC)
            lanes = slice(128 * half, 128 * half + 128)
            for i in range(mf * 2):
                member, field, part = i // (2 * fields), i // 2 % fields, i % 2
                rows = slice(SG * i, SG * i + SG)
                value = jnp.where(is_odd, odd[rows, lanes], even[rows, lanes])
                value = jnp.where(live, value, 0.0)
                start = member * 2 * fields + part * fields + field + (2 * nt + half) * SG * 2 * mf
                spec[pl.ds(start, SG, stride=2 * mf), :] = value


def spec_rows(spec, s, mf):
    tiles = [spec[pl.ds((t * SG + s) * 2 * mf, 2 * mf), :] for t in range(NPAD // 128)]
    return jnp.concatenate(tiles, axis=1).astype(BF16)


def finish_rows(base_of, noise, even_t, odd_t, wave, kids, spec_out, four_out, mf):
    w = wave.astype(jnp.int32)
    wide = jnp.concatenate([w] * (NPAD // 128), axis=1)
    for s in range(SG):
        rows = slice(s * 2 * mf, (s + 1) * 2 * mf)
        ws = wide[s : s + 1, :TRUNC]
        live = (iota((2 * mf, TRUNC), 1) >= ws) & (ws < TRUNC)
        base = base_of(s).astype(F32)[:, :TRUNC]
        child = (base + jnp.where(live, noise[rows, :].astype(F32), 0.0)).astype(BF16)
        spec_out[rows, :] = child
        kids[rows, :TRUNC] = child
        kids[rows, TRUNC:] = jnp.zeros((2 * mf, NPAD - TRUNC), BF16)
    for nt in range(NLAT // 256):
        cols = slice(256 * nt, 256 * nt + 256)
        even = lax.dot_general(kids[...], even_t[:, cols], NN, preferred_element_type=F32)
        odd = lax.dot_general(kids[...], odd_t[:, cols], NN, preferred_element_type=F32)
        for s in range(SG):
            rows = slice(s * 2 * mf, (s + 1) * 2 * mf)
            ws = jnp.concatenate([w[s : s + 1, :]] * 2, axis=1)
            is_odd = jnp.broadcast_to((ws & 1) == 1, (2 * mf, 256))
            four_out[rows, cols] = jnp.where(is_odd, odd[rows], even[rows]).astype(BF16)


def kernel(
    lat_count, member_count,
    parents_hbm, waves_row_hbm, velocity, tracer, noise,
    spec_v, four_v, last_x, last_noise, last_wave, even_t, odd_t, even_f, odd_f,
    parents, waves_row, wave_b, vel, tra, prod, table, four, low, high, sel, recv,
    xmat, spec, kids, noise_v, own_s, low_s, high_s,
    small_sem, ss_sem, sr_sem, in_sem, noise_sem, xs_sem, xr_sem, as_sem, ar_sem,
):
    me = lax.axis_index("lat")
    group = lax.axis_index("member")
    chunks = four.shape[0]
    slots_here = chunks * SG
    halves = 2
    half_count = lat_count // halves
    lat_local = NLAT // lat_count
    mf = vel.shape[0] // lat_local
    chunk_rows = SG * 2 * mf
    fields = mf // 2

    barrier = pltpu.get_barrier_semaphore()
    up = lax.rem(group + 1, member_count)
    down = lax.rem(group + member_count - 1, member_count)

    pieces = 4
    piece = vel.shape[0] // pieces

    def loads(i):
        block = pl.ds(i * piece, piece)
        return (
            pltpu.make_async_copy(velocity.at[block], vel.at[block], in_sem.at[0, i]),
            pltpu.make_async_copy(tracer.at[block], tra.at[block], in_sem.at[1, i]),
        )

    for c in loads(0):
        c.start()

    @pl.loop(1, lat_count)
    def _(o):
        pl.semaphore_signal(
            barrier, inc=1, device_id={"lat": lax.rem(me + o, lat_count)}, device_id_type=MESH
        )

    pl.semaphore_signal(barrier, inc=1, device_id={"member": up}, device_id_type=MESH)
    pl.semaphore_signal(barrier, inc=1, device_id={"member": down}, device_id_type=MESH)
    load_w = pltpu.make_async_copy(waves_row_hbm, waves_row, small_sem.at[0])
    load_w.start()
    for i in range(1, pieces):
        for c in loads(i):
            c.start()
    load_p = pltpu.make_async_copy(parents_hbm, parents, small_sem.at[1])
    load_p.start()
    load_n = pltpu.make_async_copy(noise, noise_v, noise_sem)
    load_n.start()

    y_count = 128 // lat_local
    z_count = lat_count // y_count
    my_z, my_y = me // y_count, lax.rem(me, y_count)

    def turn_of(k):
        r = z_count - 1 - k
        return (r + 1) // 2 * (1 - 2 * lax.rem(r + 1, 2))

    def target_of(i):
        z = lax.rem(my_z + turn_of(i // y_count) + z_count, z_count)
        return z * y_count + lax.rem(my_y + i + 1, y_count)

    def make_table(q, first):
        together = 4

        @pl.loop(0, half_count // together)
        def _(b):
            w = jnp.concatenate(
                [
                    wave_b[
                        pl.ds(pl.multiple_of(target_of(first + b * together + j) * slots_here + q * SG, SG), SG), :
                    ]
                    for j in range(together)
                ],
                axis=0,
            ).astype(jnp.int32)
            c, s = cos_sin((w * iota(w.shape, 1)) & (NLON - 1), NLON)
            ct, st = cos_sin((w * 128) & (NLON - 1), NLON)
            weight = jnp.where(w < TRUNC, 1.0 / math.sqrt(NLON), 0.0)
            c = c * weight
            s = -s * weight
            sign = jnp.where((w & 1) == 1, -1.0, 1.0)
            half = NLON // 2
            for t in range(half // 128):
                for factor, offset in ((None, 0), (sign, half)):
                    cc = c if factor is None else c * factor
                    ss = s if factor is None else s * factor
                    for j in range(together):
                        part = slice(j * SG, j * SG + SG)
                        rows = pl.ds(pl.multiple_of((b * together + j) * 2 * SG, 2 * SG), 2 * SG)
                        table[rows, offset + 128 * t : offset + 128 * t + 128] = jnp.concatenate(
                            [cc[part], ss[part]], axis=0
                        ).astype(BF16)
                if t + 1 < half // 128:
                    c, s = c * ct + s * st, s * ct - c * st

    def zonal(q, h):
        first = h * half_count
        make_table(q, first)
        out = lax.dot_general(table[...], prod[...], NT, preferred_element_type=F32)
        four[q, first : first + half_count] = out.astype(BF16).reshape(half_count, 2 * SG, out.shape[1])

    def make_waves():
        load_w.wait()
        for r in range(waves_row.shape[0]):
            row = waves_row[r : r + 1, :].astype(F32)
            wave_b[128 * r : 128 * r + 128, :] = jnp.transpose(jnp.broadcast_to(row, (128, 128)))

    def make_product():
        for i in range(pieces):
            for c in loads(i):
                c.wait()

            @pl.loop(0, piece // 32)
            def _(b):
                rows = pl.ds(pl.multiple_of(i * piece + b * 32, 32), 32)
                prod[rows, :] = (vel[rows, :].astype(F32) * tra[rows, :].astype(F32)).astype(BF16)

    make_waves()
    make_product()

    def x_copies(q, h):
        block = pl.ds(h * half_count, half_count)
        to_up = pltpu.make_async_remote_copy(
            src_ref=four.at[q, block], dst_ref=low.at[q, block],
            send_sem=xs_sem.at[q, h, 0], recv_sem=xr_sem.at[q, h, 0],
            device_id={"member": up}, device_id_type=MESH,
        )
        to_down = pltpu.make_async_remote_copy(
            src_ref=four.at[q, block], dst_ref=high.at[q, block],
            send_sem=xs_sem.at[q, h, 1], recv_sem=xr_sem.at[q, h, 1],
            device_id={"member": down}, device_id_type=MESH,
        )
        return to_up, to_down

    def send_half(q, h, source):
        first = h * half_count
        last = h == halves - 1

        @pl.loop(first, first + half_count - (1 if last else 0))
        def _(i):
            pltpu.make_async_remote_copy(
                src_ref=source.at[q, i], dst_ref=recv.at[q, me],
                send_sem=as_sem.at[q], recv_sem=ar_sem.at[q, my_z],
                device_id={"lat": target_of(i)}, device_id_type=MESH,
            ).start()

        if last:
            recv[q, me] = source[q, lat_count - 1]

    zonal(0, 0)
    pl.semaphore_wait(barrier, lat_count + 1)
    send_half(0, 0, four)
    zonal(0, 1)
    send_half(0, 1, four)
    for q in range(1, chunks):
        for h in range(halves):
            zonal(q, h)
            for c in x_copies(q, h):
                c.start()

    def make_basis(even, odd, rows_are_degrees):
        step = 64
        period = 4 * NLAT
        row_count, lane_count = even.shape
        lanes = lane_count // (2 if rows_are_degrees else 3)
        scale = math.sqrt(2.0 / NLAT)

        @pl.loop(0, lane_count // lanes)
        def _(tile):
            lane = tile * lanes + iota((8, lanes), 1)
            sub = iota((8, lanes), 0)
            turn = 8 * (2 * lane + 1) if rows_are_degrees else 16 * lane
            c8, s8 = cos_sin(turn & (period - 1), period)
            cols = pl.ds(pl.multiple_of(tile * lanes, 128), lanes)

            @pl.loop(0, row_count // step)
            def _(a):
                row = a * step + sub
                phase = row * (2 * lane + 1) if rows_are_degrees else lane * (2 * row + 1)
                c, s = cos_sin(phase & (period - 1), period)
                c = c * scale
                s = s * scale
                for b in range(step // 16):
                    c2, s2 = c * c8 - s * s8, s * c8 + c * s8
                    r16 = pl.ds(pl.multiple_of(a * step + b * 16, 16), 16)
                    even[r16, cols] = jnp.concatenate([c, c2], axis=0).astype(BF16)
                    odd[r16, cols] = jnp.concatenate([s, s2], axis=0).astype(BF16)
                    c, s = c2 * c8 - s2 * s8, s2 * c8 + c2 * s8

    load_p.wait()
    first_member = group * 2
    places = [parents[first_member + m] - first_member + SPREAD for m in range(2)]

    def select_half(q, h):
        width = fields * lat_local

        @pl.loop(h * half_count, (h + 1) * half_count)
        def _(i):
            for m in range(2):
                chosen = None
                for p in range(m, m + 2 * SPREAD + 1):
                    source = (low, four, high)[p // 2]
                    cand = source[q, i, :, (p % 2) * width : (p % 2 + 1) * width]
                    hit = jnp.broadcast_to(places[m] == p, cand.shape)
                    chosen = cand if chosen is None else jnp.where(hit, cand, chosen)
                sel[q, i, :, m * width : (m + 1) * width] = chosen

    def relay(q, h):
        for c in x_copies(q, h):
            c.wait_recv()
        select_half(q, h)
        send_half(q, h, sel)

    for q in range(1, chunks):
        for h in range(halves):
            relay(q, h)

    make_basis(even_f, odd_f, False)
    make_basis(even_t, odd_t, True)
    load_n.wait()

    def arrive(q, p, count):
        block = recv.at[q, pl.ds(p * y_count, count)]
        pltpu.make_async_remote_copy(
            src_ref=block, dst_ref=block, send_sem=as_sem.at[q], recv_sem=ar_sem.at[q, p],
            device_id={"lat": me}, device_id_type=MESH,
        ).wait_recv()

    def shuffle(q, xmat):
        per = 128 // lat_local
        lane = iota((2 * SG, 128), 1) // lat_local
        low_half = lane < 2
        even_block = (lane & 1) == 0

        def swap(x, y, mask, width):
            left = jnp.where(mask, x, pltpu.roll(y, width, 1))
            right = jnp.where(mask, pltpu.roll(x, 128 - width, 1), y)
            return left, right

        def arrange(p):
            target = pl.ds(pl.multiple_of(p * 128, 128), 128)
            for t in range(mf // per):
                x0, x1, x2, x3 = [recv[q, p * per + i, :, 128 * t : 128 * t + 128] for i in range(per)]
                x0, x2 = swap(x0, x2, low_half, 2 * lat_local)
                x1, x3 = swap(x1, x3, low_half, 2 * lat_local)
                x0, x1 = swap(x0, x1, even_block, lat_local)
                x2, x3 = swap(x2, x3, even_block, lat_local)
                for k, x in enumerate((x0, x1, x2, x3)):
                    xmat[(t * per + k) * 2 * SG : (t * per + k + 1) * 2 * SG, target] = x

        @pl.loop(0, z_count - 1)
        def _(k):
            p = lax.rem(my_z - turn_of(k) + z_count, z_count)
            arrive(q, p, per)
            arrange(p)

        arrive(q, my_z, per - 1)
        arrange(my_z)

    def forward(q):
        shuffle(q, xmat)
        product(q)

    def own_wave(q):
        return wave_b[pl.ds(pl.multiple_of(me * slots_here + q * SG, SG), SG), :]

    def product(q):
        forward_rows(xmat, even_f, odd_f, own_wave(q), spec, mf)

    def finish(q, base_of):
        block = pl.ds(q * chunk_rows, chunk_rows)
        finish_rows(
            base_of, noise_v.at[block], even_t, odd_t, own_wave(q), kids,
            spec_v.at[block], four_v.at[block], mf,
        )

    def own_of(s):
        return spec_rows(spec, s, mf)

    def s_copies():
        to_up = pltpu.make_async_remote_copy(
            src_ref=own_s, dst_ref=low_s, send_sem=ss_sem.at[0], recv_sem=sr_sem.at[0],
            device_id={"member": up}, device_id_type=MESH,
        )
        to_down = pltpu.make_async_remote_copy(
            src_ref=own_s, dst_ref=high_s, send_sem=ss_sem.at[1], recv_sem=sr_sem.at[1],
            device_id={"member": down}, device_id_type=MESH,
        )
        return to_up, to_down

    def share():
        for s in range(SG):
            own_s[s * 2 * mf : (s + 1) * 2 * mf, :] = own_of(s)
        for c in s_copies():
            c.start()

    def chosen_of(s):
        out = []
        for m in range(2):
            chosen = None
            for p in range(m, m + 2 * SPREAD + 1):
                source = (low_s, own_s, high_s)[p // 2]
                start = s * 2 * mf + (p % 2) * mf
                cand = source[start : start + mf, :]
                hit = jnp.broadcast_to(places[m] == p, cand.shape)
                chosen = cand if chosen is None else jnp.where(hit, cand, chosen)
            out.append(chosen)
        return jnp.concatenate(out, axis=0)

    forward(0)
    share()
    forward(1)
    finish(1, own_of)
    for c in s_copies():
        c.wait_recv()
    finish(0, chosen_of)
    last_noise[...] = noise_v[2 * chunk_rows : 3 * chunk_rows, :]
    last_wave[...] = own_wave(2)
    shuffle(2, last_x)

    for c in s_copies():
        c.wait_send()
    for q in range(chunks):
        if q > 0:
            for h in range(halves):
                for c in x_copies(q, h):
                    c.wait_send()
        pltpu.make_async_remote_copy(
            src_ref=sel.at[q, pl.ds(0, lat_count - 1)], dst_ref=recv.at[q, pl.ds(0, lat_count - 1)],
            send_sem=as_sem.at[q], recv_sem=ar_sem.at[q, 0], device_id={"lat": me}, device_id_type=MESH,
        ).wait_send()


def tail(mf, spec_v, four_v, x, noise, wave, even_t, odd_t, even_f, odd_f, spectra_out, fourier_out, spec, kids, spec_l, four_l, sem):
    done = spec_v.shape[0]
    rows = x.shape[0]
    early = (
        pltpu.make_async_copy(spec_v, spectra_out.at[pl.ds(0, done)], sem.at[0]),
        pltpu.make_async_copy(four_v, fourier_out.at[pl.ds(0, done)], sem.at[1]),
    )
    for c in early:
        c.start()
    w = wave[...]
    forward_rows(x, even_f, odd_f, w, spec, mf)
    finish_rows(lambda s: spec_rows(spec, s, mf), noise, even_t, odd_t, w, kids, spec_l, four_l, mf)
    late = (
        pltpu.make_async_copy(spec_l, spectra_out.at[pl.ds(done, rows)], sem.at[2]),
        pltpu.make_async_copy(four_l, fourier_out.at[pl.ds(done, rows)], sem.at[3]),
    )
    for c in late:
        c.start()
    for c in early + late:
        c.wait()


def per_device(lat_count, member_count, velocity, tracer, wave_slots, parents, noise):
    mem, fields, lat_local, lon = velocity.shape
    slots = wave_slots.shape[0]
    here = slots // lat_count
    chunks = here // SG
    rows = mem * fields * lat_local
    mf = mem * fields
    out_rows = here * mem * 2 * fields
    chunk_rows = SG * 2 * mf
    msg = (chunks, lat_count, 2 * SG, rows)
    dma = pltpu.SemaphoreType.DMA
    hbm = pl.BlockSpec(memory_space=pltpu.HBM)
    vmem = pl.BlockSpec(memory_space=pltpu.VMEM)
    early = out_rows - chunk_rows
    middle = (
        jax.ShapeDtypeStruct((early, TRUNC), BF16),
        jax.ShapeDtypeStruct((early, NLAT), BF16),
        jax.ShapeDtypeStruct((chunk_rows, NLAT), BF16),
        jax.ShapeDtypeStruct((chunk_rows, TRUNC), BF16),
        jax.ShapeDtypeStruct((SG, 128), F32),
        jax.ShapeDtypeStruct((NPAD, NLAT), BF16),
        jax.ShapeDtypeStruct((NPAD, NLAT), BF16),
        jax.ShapeDtypeStruct((NLAT, NPAD), BF16),
        jax.ShapeDtypeStruct((NLAT, NPAD), BF16),
    )
    parts = pl.pallas_call(
        functools.partial(kernel, lat_count, member_count),
        out_shape=middle,
        in_specs=[hbm] * 5,
        out_specs=(vmem,) * len(middle),
        scratch_shapes=[
            pltpu.SMEM(parents.shape, jnp.int32),
            pltpu.VMEM((slots // 128, 128), jnp.int32),
            pltpu.VMEM((slots, 128), F32),
            pltpu.VMEM((rows, lon), BF16),
            pltpu.VMEM((rows, lon), BF16),
            pltpu.VMEM((rows, lon), BF16),
            pltpu.VMEM((lat_count // 2 * 2 * SG, lon), BF16),
            pltpu.VMEM(msg, BF16),
            pltpu.VMEM(msg, BF16),
            pltpu.VMEM(msg, BF16),
            pltpu.VMEM(msg, BF16),
            pltpu.VMEM(msg, BF16),
            pltpu.VMEM((chunk_rows, NLAT), BF16),
            pltpu.VMEM((NPAD // 128 * chunk_rows, 128), F32),
            pltpu.VMEM((chunk_rows, NPAD), BF16),
            pltpu.VMEM((out_rows, TRUNC), BF16),
            pltpu.VMEM((chunk_rows, NPAD), BF16),
            pltpu.VMEM((chunk_rows, NPAD), BF16),
            pltpu.VMEM((chunk_rows, NPAD), BF16),
            dma((2,)),
            dma((2,)),
            dma((2,)),
            dma((2, 4)),
            dma,
            dma((chunks, 2, 2)),
            dma((chunks, 2, 2)),
            dma((chunks,)),
            dma((chunks, lat_count * lat_local // 128)),
        ],
        compiler_params=pltpu.CompilerParams(
            collective_id=0, has_side_effects=True, vmem_limit_bytes=44 * 1024 * 1024
        ),
        name="transform",
    )(
        pltpu.with_memory_space_constraint(parents, pltpu.HBM),
        pltpu.with_memory_space_constraint(wave_slots.reshape(slots // 128, 128), pltpu.HBM),
        pltpu.with_memory_space_constraint(velocity.reshape(rows, lon), pltpu.HBM),
        pltpu.with_memory_space_constraint(tracer.reshape(rows, lon), pltpu.HBM),
        pltpu.with_memory_space_constraint(noise.reshape(out_rows, TRUNC), pltpu.HBM),
    )
    spectra, fourier = pl.pallas_call(
        functools.partial(tail, mf),
        out_shape=(
            jax.ShapeDtypeStruct((out_rows, TRUNC), BF16),
            jax.ShapeDtypeStruct((out_rows, NLAT), BF16),
        ),
        in_specs=[vmem] * len(middle),
        out_specs=(hbm, hbm),
        scratch_shapes=[
            pltpu.VMEM((NPAD // 128 * chunk_rows, 128), F32),
            pltpu.VMEM((chunk_rows, NPAD), BF16),
            pltpu.VMEM((chunk_rows, TRUNC), BF16),
            pltpu.VMEM((chunk_rows, NLAT), BF16),
            dma((4,)),
        ],
        compiler_params=pltpu.CompilerParams(vmem_limit_bytes=44 * 1024 * 1024),
        name="last",
    )(*parts)
    return (
        spectra.reshape(here, mem, 2, fields, TRUNC),
        fourier.reshape(here, mem, 2, fields, NLAT),
    )


def solution(mesh):
    in_specs = (
        P("member", None, "lat", None),
        P("member", None, "lat", None),
        P(),
        P(),
        P("lat", "member", None, None, None),
    )
    out_specs = (P("lat", "member", None, None, None), P("lat", "member", None, None, None))
    return jax.shard_map(
        functools.partial(per_device, mesh.shape["lat"], mesh.shape["member"]),
        mesh=mesh, in_specs=in_specs, out_specs=out_specs, check_vma=False,
    )
```

```python
import functools
import math

import jax
import jax.numpy as jnp
from jax import lax
from jax.experimental import pallas as pl
from jax.experimental.pallas import tpu as pltpu
from jax.sharding import PartitionSpec as P

NLAT = 1024
NLON = 2048
TRUNC = 683
NPAD = 768
SPREAD = 2
SG = 8
MESH = pl.DeviceIdType.MESH
F32 = jnp.float32
BF16 = jnp.bfloat16
NT = (((1,), (1,)), ((), ()))
NN = (((1,), (0,)), ((), ()))


def iota(shape, dim):
    return lax.broadcasted_iota(jnp.int32, shape, dim)


def cos_sin(phase, period):
    eighth = period // 8
    quarter = period // 4
    shifted = phase + eighth
    quad = (shifted // quarter) & 3
    x = ((shifted & (quarter - 1)) - eighth).astype(F32) * (2.0 * math.pi / period)
    y = x * x
    s = x * (1.0 + y * (-1.0 / 6 + y * (1.0 / 120 + y * (-1.0 / 5040 + y * (1.0 / 362880)))))
    c = 1.0 + y * (-0.5 + y * (1.0 / 24 + y * (-1.0 / 720 + y * (1.0 / 40320))))
    odd = (quad & 1) == 1
    cos = jnp.where(odd, s, c)
    sin = jnp.where(odd, c, s)
    cos = jnp.where((quad == 1) | (quad == 2), -cos, cos)
    sin = jnp.where(quad >= 2, -sin, sin)
    return cos, sin


def by_parity(x, even_f, odd_f, cols, is_odd):
    even = lax.dot_general(x, even_f[:, cols], NN, preferred_element_type=F32)
    odd = lax.dot_general(x, odd_f[:, cols], NN, preferred_element_type=F32)
    out = []
    for half in range(2):
        lanes = slice(128 * half, 128 * half + 128)
        groups = range(0, x.shape[0], SG)
        out.append([jnp.where(is_odd, odd[i : i + SG, lanes], even[i : i + SG, lanes]) for i in groups])
    return out


def partial_rows(x, even_f, odd_f, wave, acc):
    is_odd = (wave.astype(jnp.int32) & 1) == 1
    for nt in range(NPAD // 256):
        cols = slice(256 * nt, 256 * nt + 256)
        for half, groups in enumerate(by_parity(x, even_f, odd_f, cols, is_odd)):
            start = 256 * nt + 128 * half
            acc[:, start : start + 128] = jnp.concatenate(groups, axis=0)


def forward_rows(x, even_f, odd_f, wave, order, acc, spec):
    w = wave.astype(jnp.int32)
    is_odd = (w & 1) == 1
    for nt in range(NPAD // 256):
        cols = slice(256 * nt, 256 * nt + 256)
        tiles = []
        for half, groups in enumerate(by_parity(x, even_f, odd_f, cols, is_odd)):
            start = 256 * nt + 128 * half
            n = start + iota((SG, 128), 1)
            live = (n >= w) & (w < TRUNC) & (n < TRUNC)
            if acc is not None:
                groups = [g + acc[SG * i : SG * i + SG, start : start + 128] for i, g in enumerate(groups)]
            tiles.append(jnp.concatenate([jnp.where(live, g, 0.0) for g in groups], axis=0))
        value = jnp.concatenate(tiles, axis=1).astype(BF16)
        spec[:, cols] = lax.dot_general(order, value, NN, preferred_element_type=F32).astype(BF16)


def finish_rows(base_of, noise, even_t, odd_t, wave, kids, spec_out, four_out, mf, ready=lambda part: None):
    w = wave.astype(jnp.int32)
    wide = jnp.concatenate([w] * (NPAD // 128), axis=1)
    for s in range(SG):
        rows = slice(s * 2 * mf, (s + 1) * 2 * mf)
        ws = wide[s : s + 1, :TRUNC]
        live = (iota((2 * mf, TRUNC), 1) >= ws) & (ws < TRUNC)
        base = base_of(s).astype(F32)[:, :TRUNC]
        child = (base + jnp.where(live, noise[rows, :].astype(F32), 0.0)).astype(BF16)
        spec_out[rows, :] = child
        kids[rows, :TRUNC] = child
        kids[rows, TRUNC:] = jnp.zeros((2 * mf, NPAD - TRUNC), BF16)
    ready(0)
    for nt in range(NLAT // 256):
        cols = slice(256 * nt, 256 * nt + 256)
        even = lax.dot_general(kids[...], even_t[:, cols], NN, preferred_element_type=F32)
        odd = lax.dot_general(kids[...], odd_t[:, cols], NN, preferred_element_type=F32)
        for s in range(SG):
            rows = slice(s * 2 * mf, (s + 1) * 2 * mf)
            ws = jnp.concatenate([w[s : s + 1, :]] * 2, axis=1)
            is_odd = jnp.broadcast_to((ws & 1) == 1, (2 * mf, 256))
            four_out[rows, cols] = jnp.where(is_odd, odd[rows], even[rows]).astype(BF16)
        ready(nt + 1)


def kernel(
    lat_count, member_count,
    parents_hbm, waves_row_hbm, velocity, tracer, noise,
    spec_v, four_v, acc, last_x, last_noise, last_wave, order, even_t, odd_t, even_l, odd_l,
    parents, waves_row, wave_b, vel, tra, prod, table, four, low, high, sel, recv,
    even_f, odd_f, xmat, spec, kids, noise_v, own_s, low_s, high_s,
    small_sem, ss_sem, sr_sem, in_sem, noise_sem, xs_sem, xr_sem, as_sem, ar_sem,
):
    me = lax.axis_index("lat")
    group = lax.axis_index("member")
    chunks = four.shape[0]
    slots_here = chunks * SG
    halves = 2
    half_count = lat_count // halves
    lat_local = NLAT // lat_count
    mf = vel.shape[0] // lat_local
    chunk_rows = SG * 2 * mf
    fields = mf // 2

    barrier = pltpu.get_barrier_semaphore()
    up = lax.rem(group + 1, member_count)
    down = lax.rem(group + member_count - 1, member_count)

    pieces = 4
    piece = vel.shape[0] // pieces

    def loads(i):
        block = pl.ds(i * piece, piece)
        return (
            pltpu.make_async_copy(velocity.at[block], vel.at[block], in_sem.at[0, i]),
            pltpu.make_async_copy(tracer.at[block], tra.at[block], in_sem.at[1, i]),
        )

    for c in loads(0):
        c.start()

    @pl.loop(1, lat_count)
    def _(o):
        pl.semaphore_signal(
            barrier, inc=1, device_id={"lat": lax.rem(me + o, lat_count)}, device_id_type=MESH
        )

    pl.semaphore_signal(barrier, inc=1, device_id={"member": up}, device_id_type=MESH)
    pl.semaphore_signal(barrier, inc=1, device_id={"member": down}, device_id_type=MESH)
    load_w = pltpu.make_async_copy(waves_row_hbm, waves_row, small_sem.at[0])
    load_w.start()
    for i in range(1, pieces):
        for c in loads(i):
            c.start()
    load_p = pltpu.make_async_copy(parents_hbm, parents, small_sem.at[1])
    load_p.start()
    load_n = pltpu.make_async_copy(noise, noise_v, noise_sem)
    load_n.start()

    y_count = 128 // lat_local
    z_count = lat_count // y_count
    my_z, my_y = me // y_count, lax.rem(me, y_count)

    def turn_of(k):
        r = z_count - 1 - k
        return (r + 1) // 2 * (1 - 2 * lax.rem(r + 1, 2))

    def target_of(q, i):
        if q < chunks - 1:
            k, y = lax.rem(i, z_count), i // z_count + 1
        else:
            k, y = i // y_count, i + 1
        z = lax.rem(my_z + turn_of(k) + z_count, z_count)
        return z * y_count + lax.rem(my_y + y, y_count)

    def make_table(q, first):
        together = 4

        @pl.loop(0, half_count // together)
        def _(b):
            w = jnp.concatenate(
                [
                    wave_b[
                        pl.ds(pl.multiple_of(target_of(q, first + b * together + j) * slots_here + q * SG, SG), SG), :
                    ]
                    for j in range(together)
                ],
                axis=0,
            ).astype(jnp.int32)
            c, s = cos_sin((w * iota(w.shape, 1)) & (NLON - 1), NLON)
            ct, st = cos_sin((w * 128) & (NLON - 1), NLON)
            weight = jnp.where(w < TRUNC, 1.0 / math.sqrt(NLON), 0.0)
            c = c * weight
            s = -s * weight
            sign = jnp.where((w & 1) == 1, -1.0, 1.0)
            half = NLON // 2
            for t in range(half // 128):
                for factor, offset in ((None, 0), (sign, half)):
                    cc = c if factor is None else c * factor
                    ss = s if factor is None else s * factor
                    for j in range(together):
                        part = slice(j * SG, j * SG + SG)
                        rows = pl.ds(pl.multiple_of((b * together + j) * 2 * SG, 2 * SG), 2 * SG)
                        table[rows, offset + 128 * t : offset + 128 * t + 128] = jnp.concatenate(
                            [cc[part], ss[part]], axis=0
                        ).astype(BF16)
                if t + 1 < half // 128:
                    c, s = c * ct + s * st, s * ct - c * st

    def zonal(q, h):
        first = h * half_count
        make_table(q, first)
        out = lax.dot_general(table[...], prod[...], NT, preferred_element_type=F32)
        four[q, first : first + half_count] = out.astype(BF16).reshape(half_count, 2 * SG, out.shape[1])

    def make_waves():
        load_w.wait()
        for r in range(waves_row.shape[0]):
            row = waves_row[r : r + 1, :].astype(F32)
            wave_b[128 * r : 128 * r + 128, :] = jnp.transpose(jnp.broadcast_to(row, (128, 128)))

    def make_product():
        for i in range(pieces):
            for c in loads(i):
                c.wait()

            @pl.loop(0, piece // 32)
            def _(b):
                rows = pl.ds(pl.multiple_of(i * piece + b * 32, 32), 32)
                prod[rows, :] = (vel[rows, :].astype(F32) * tra[rows, :].astype(F32)).astype(BF16)

    make_waves()
    make_product()

    def x_copies(q, h):
        block = pl.ds(h * half_count, half_count)
        to_up = pltpu.make_async_remote_copy(
            src_ref=four.at[q, block], dst_ref=low.at[q, block],
            send_sem=xs_sem.at[q, h, 0], recv_sem=xr_sem.at[q, h, 0],
            device_id={"member": up}, device_id_type=MESH,
        )
        to_down = pltpu.make_async_remote_copy(
            src_ref=four.at[q, block], dst_ref=high.at[q, block],
            send_sem=xs_sem.at[q, h, 1], recv_sem=xr_sem.at[q, h, 1],
            device_id={"member": down}, device_id_type=MESH,
        )
        return to_up, to_down

    def send_half(q, h, source):
        first = h * half_count
        last = h == halves - 1

        @pl.loop(first, first + half_count - (1 if last else 0))
        def _(i):
            pltpu.make_async_remote_copy(
                src_ref=source.at[q, i], dst_ref=recv.at[q, me],
                send_sem=as_sem.at[q], recv_sem=ar_sem.at[q, my_z],
                device_id={"lat": target_of(q, i)}, device_id_type=MESH,
            ).start()

        if last:
            recv[q, me] = source[q, lat_count - 1]

    zonal(0, 0)
    pl.semaphore_wait(barrier, lat_count + 1)
    send_half(0, 0, four)
    zonal(0, 1)
    send_half(0, 1, four)
    for q in range(1, chunks):
        for h in range(halves):
            zonal(q, h)
            for c in x_copies(q, h):
                c.start()

    def source_of(k):
        return lax.rem(my_z - turn_of(k) + z_count, z_count)

    def make_order():
        row = iota(order.shape, 0)
        col = iota(order.shape, 1)
        slot, member, part, field = row // (2 * mf), row // mf % 2, row // fields % 2, row % fields
        source = ((member * fields + field) * 2 + part) * SG + slot
        order[...] = jnp.where(col == source, 1.0, 0.0).astype(BF16)

    def make_basis(even, odd, rows_are_degrees):
        step = 64
        period = 4 * NLAT
        row_count, lane_count = even.shape
        lanes = lane_count // (2 if rows_are_degrees else 3)
        scale = math.sqrt(2.0 / NLAT)

        @pl.loop(0, lane_count // lanes)
        def _(tile):
            lane = tile * lanes + iota((8, lanes), 1)
            sub = iota((8, lanes), 0)
            turn = 8 * (2 * lane + 1) if rows_are_degrees else 16 * lane
            c8, s8 = cos_sin(turn & (period - 1), period)
            cols = pl.ds(pl.multiple_of(tile * lanes, 128), lanes)

            @pl.loop(0, row_count // step)
            def _(a):
                row = a * step + sub
                if not rows_are_degrees:
                    row = row + (source_of(a // 2) - a // 2) * 128
                phase = row * (2 * lane + 1) if rows_are_degrees else lane * (2 * row + 1)
                c, s = cos_sin(phase & (period - 1), period)
                c = c * scale
                s = s * scale
                for b in range(step // 16):
                    c2, s2 = c * c8 - s * s8, s * c8 + c * s8
                    r16 = pl.ds(pl.multiple_of(a * step + b * 16, 16), 16)
                    even[r16, cols] = jnp.concatenate([c, c2], axis=0).astype(BF16)
                    odd[r16, cols] = jnp.concatenate([s, s2], axis=0).astype(BF16)
                    c, s = c2 * c8 - s2 * s8, s2 * c8 + c2 * s8

    load_p.wait()
    first_member = group * 2
    places = [parents[first_member + m] - first_member + SPREAD for m in range(2)]

    def select_half(q, h):
        width = fields * lat_local

        @pl.loop(h * half_count, (h + 1) * half_count)
        def _(i):
            for m in range(2):
                chosen = None
                for p in range(m, m + 2 * SPREAD + 1):
                    source = (low, four, high)[p // 2]
                    cand = source[q, i, :, (p % 2) * width : (p % 2 + 1) * width]
                    hit = jnp.broadcast_to(places[m] == p, cand.shape)
                    chosen = cand if chosen is None else jnp.where(hit, cand, chosen)
                sel[q, i, :, m * width : (m + 1) * width] = chosen

    def relay(q, h):
        for c in x_copies(q, h):
            c.wait_recv()
        select_half(q, h)
        send_half(q, h, sel)

    relay(1, 0)
    make_basis(even_f, odd_f, False)
    relay(1, 1)
    make_basis(even_t, odd_t, True)
    relay(2, 0)
    make_order()
    relay(2, 1)

    load_n.wait()

    def arrive(q, p, count):
        block = recv.at[q, pl.ds(p * y_count, count)]
        pltpu.make_async_remote_copy(
            src_ref=block, dst_ref=block, send_sem=as_sem.at[q], recv_sem=ar_sem.at[q, p],
            device_id={"lat": me}, device_id_type=MESH,
        ).wait_recv()

    split = z_count - 2

    def shuffle(q, begin, end):
        per = 128 // lat_local
        lane = iota((2 * SG, 128), 1) // lat_local
        low_half = lane < 2
        even_block = (lane & 1) == 0

        def swap(x, y, mask, width):
            left = jnp.where(mask, x, pltpu.roll(y, width, 1))
            right = jnp.where(mask, pltpu.roll(x, 128 - width, 1), y)
            return left, right

        def arrange(p, k):
            target = pl.ds(pl.multiple_of(k * 128, 128), 128)
            for t in range(mf // per):
                x0, x1, x2, x3 = [recv[q, p * per + i, :, 128 * t : 128 * t + 128] for i in range(per)]
                x0, x2 = swap(x0, x2, low_half, 2 * lat_local)
                x1, x3 = swap(x1, x3, low_half, 2 * lat_local)
                x0, x1 = swap(x0, x1, even_block, lat_local)
                x2, x3 = swap(x2, x3, even_block, lat_local)
                for j, x in enumerate((x0, x1, x2, x3)):
                    xmat[(t * per + j) * 2 * SG : (t * per + j + 1) * 2 * SG, target] = x

        @pl.loop(begin, min(end, z_count - 1))
        def _(k):
            p = source_of(k)
            arrive(q, p, per)
            arrange(p, k)

        if end == z_count:
            arrive(q, my_z, per - 1)
            arrange(my_z, z_count - 1)

    def forward(q):
        shuffle(q, 0, z_count)
        product(q)

    def own_wave(q):
        return wave_b[pl.ds(pl.multiple_of(me * slots_here + q * SG, SG), SG), :]

    def product(q):
        forward_rows(xmat[...], even_f, odd_f, own_wave(q), order[...], None, spec)

    def finish(q, base_of):
        block = pl.ds(q * chunk_rows, chunk_rows)
        finish_rows(
            base_of, noise_v.at[block], even_t, odd_t, own_wave(q), kids,
            spec_v.at[block], four_v.at[block], mf,
        )

    def own_of(s):
        return spec[s * 2 * mf : (s + 1) * 2 * mf, :]

    def s_copies():
        to_up = pltpu.make_async_remote_copy(
            src_ref=own_s, dst_ref=low_s, send_sem=ss_sem.at[0], recv_sem=sr_sem.at[0],
            device_id={"member": up}, device_id_type=MESH,
        )
        to_down = pltpu.make_async_remote_copy(
            src_ref=own_s, dst_ref=high_s, send_sem=ss_sem.at[1], recv_sem=sr_sem.at[1],
            device_id={"member": down}, device_id_type=MESH,
        )
        return to_up, to_down

    def share():
        for s in range(SG):
            own_s[s * 2 * mf : (s + 1) * 2 * mf, :] = own_of(s)
        for c in s_copies():
            c.start()

    def chosen_of(s):
        out = []
        for m in range(2):
            chosen = None
            for p in range(m, m + 2 * SPREAD + 1):
                source = (low_s, own_s, high_s)[p // 2]
                start = s * 2 * mf + (p % 2) * mf
                cand = source[start : start + mf, :]
                hit = jnp.broadcast_to(places[m] == p, cand.shape)
                chosen = cand if chosen is None else jnp.where(hit, cand, chosen)
            out.append(chosen)
        return jnp.concatenate(out, axis=0)

    forward(0)
    share()
    forward(1)
    finish(1, own_of)
    for c in s_copies():
        c.wait_recv()
    finish(0, chosen_of)
    last_noise[...] = noise_v[2 * chunk_rows : 3 * chunk_rows, :]
    last_wave[...] = own_wave(2)
    even_l[...] = even_f[split * 128 :, :]
    odd_l[...] = odd_f[split * 128 :, :]
    shuffle(2, 0, split)
    early = pl.ds(0, split * 128)
    partial_rows(xmat[:, :split * 128], even_f.at[early], odd_f.at[early], own_wave(2), acc)
    shuffle(2, split, z_count)
    last_x[...] = xmat[:, split * 128 :]

    for c in s_copies():
        c.wait_send()
    for q in range(chunks):
        if q > 0:
            for h in range(halves):
                for c in x_copies(q, h):
                    c.wait_send()
        pltpu.make_async_remote_copy(
            src_ref=sel.at[q, pl.ds(0, lat_count - 1)], dst_ref=recv.at[q, pl.ds(0, lat_count - 1)],
            send_sem=as_sem.at[q], recv_sem=ar_sem.at[q, 0], device_id={"lat": me}, device_id_type=MESH,
        ).wait_send()


def tail(
    mf, spec_v, four_v, acc, x, noise, wave, order, even_t, odd_t, even_l, odd_l,
    spectra_out, fourier_out, spec, kids, spec_l, four_l, sem,
):
    done = spec_v.shape[0]
    rows = x.shape[0]
    copies = [
        pltpu.make_async_copy(spec_v, spectra_out.at[pl.ds(0, done)], sem.at[0]),
        pltpu.make_async_copy(four_v, fourier_out.at[pl.ds(0, done)], sem.at[1]),
    ]
    for c in copies:
        c.start()
    w = wave[...]
    forward_rows(x[...], even_l, odd_l, w, order[...], acc, spec)

    def ready(part):
        if part == 0:
            c = pltpu.make_async_copy(spec_l, spectra_out.at[pl.ds(done, rows)], sem.at[2])
        else:
            cols = pl.ds(256 * (part - 1), 256)
            c = pltpu.make_async_copy(four_l.at[:, cols], fourier_out.at[pl.ds(done, rows), cols], sem.at[2 + part])
        copies.append(c)
        c.start()

    finish_rows(
        lambda s: spec[s * 2 * mf : (s + 1) * 2 * mf, :], noise, even_t, odd_t, w, kids, spec_l, four_l, mf, ready
    )
    for c in copies:
        c.wait()


def per_device(lat_count, member_count, velocity, tracer, wave_slots, parents, noise):
    mem, fields, lat_local, lon = velocity.shape
    slots = wave_slots.shape[0]
    here = slots // lat_count
    chunks = here // SG
    rows = mem * fields * lat_local
    mf = mem * fields
    out_rows = here * mem * 2 * fields
    chunk_rows = SG * 2 * mf
    msg = (chunks, lat_count, 2 * SG, rows)
    dma = pltpu.SemaphoreType.DMA
    hbm = pl.BlockSpec(memory_space=pltpu.HBM)
    vmem = pl.BlockSpec(memory_space=pltpu.VMEM)
    early = out_rows - chunk_rows
    middle = (
        jax.ShapeDtypeStruct((early, TRUNC), BF16),
        jax.ShapeDtypeStruct((early, NLAT), BF16),
        jax.ShapeDtypeStruct((chunk_rows, NPAD), F32),
        jax.ShapeDtypeStruct((chunk_rows, 256), BF16),
        jax.ShapeDtypeStruct((chunk_rows, TRUNC), BF16),
        jax.ShapeDtypeStruct((SG, 128), F32),
        jax.ShapeDtypeStruct((chunk_rows, chunk_rows), BF16),
        jax.ShapeDtypeStruct((NPAD, NLAT), BF16),
        jax.ShapeDtypeStruct((NPAD, NLAT), BF16),
        jax.ShapeDtypeStruct((256, NPAD), BF16),
        jax.ShapeDtypeStruct((256, NPAD), BF16),
    )
    parts = pl.pallas_call(
        functools.partial(kernel, lat_count, member_count),
        out_shape=middle,
        in_specs=[hbm] * 5,
        out_specs=(vmem,) * len(middle),
        scratch_shapes=[
            pltpu.SMEM(parents.shape, jnp.int32),
            pltpu.VMEM((slots // 128, 128), jnp.int32),
            pltpu.VMEM((slots, 128), F32),
            pltpu.VMEM((rows, lon), BF16),
            pltpu.VMEM((rows, lon), BF16),
            pltpu.VMEM((rows, lon), BF16),
            pltpu.VMEM((lat_count // 2 * 2 * SG, lon), BF16),
            pltpu.VMEM(msg, BF16),
            pltpu.VMEM(msg, BF16),
            pltpu.VMEM(msg, BF16),
            pltpu.VMEM(msg, BF16),
            pltpu.VMEM(msg, BF16),
            pltpu.VMEM((NLAT, NPAD), BF16),
            pltpu.VMEM((NLAT, NPAD), BF16),
            pltpu.VMEM((chunk_rows, NLAT), BF16),
            pltpu.VMEM((chunk_rows, NPAD), BF16),
            pltpu.VMEM((chunk_rows, NPAD), BF16),
            pltpu.VMEM((out_rows, TRUNC), BF16),
            pltpu.VMEM((chunk_rows, NPAD), BF16),
            pltpu.VMEM((chunk_rows, NPAD), BF16),
            pltpu.VMEM((chunk_rows, NPAD), BF16),
            dma((2,)),
            dma((2,)),
            dma((2,)),
            dma((2, 4)),
            dma,
            dma((chunks, 2, 2)),
            dma((chunks, 2, 2)),
            dma((chunks,)),
            dma((chunks, lat_count * lat_local // 128)),
        ],
        compiler_params=pltpu.CompilerParams(
            collective_id=0, has_side_effects=True, vmem_limit_bytes=44 * 1024 * 1024
        ),
        name="transform",
    )(
        pltpu.with_memory_space_constraint(parents, pltpu.HBM),
        pltpu.with_memory_space_constraint(wave_slots.reshape(slots // 128, 128), pltpu.HBM),
        pltpu.with_memory_space_constraint(velocity.reshape(rows, lon), pltpu.HBM),
        pltpu.with_memory_space_constraint(tracer.reshape(rows, lon), pltpu.HBM),
        pltpu.with_memory_space_constraint(noise.reshape(out_rows, TRUNC), pltpu.HBM),
    )
    spectra, fourier = pl.pallas_call(
        functools.partial(tail, mf),
        out_shape=(
            jax.ShapeDtypeStruct((out_rows, TRUNC), BF16),
            jax.ShapeDtypeStruct((out_rows, NLAT), BF16),
        ),
        in_specs=[vmem] * len(middle),
        out_specs=(hbm, hbm),
        scratch_shapes=[
            pltpu.VMEM((chunk_rows, NPAD), BF16),
            pltpu.VMEM((chunk_rows, NPAD), BF16),
            pltpu.VMEM((chunk_rows, TRUNC), BF16),
            pltpu.VMEM((chunk_rows, NLAT), BF16),
            dma((3 + NLAT // 256,)),
        ],
        compiler_params=pltpu.CompilerParams(vmem_limit_bytes=44 * 1024 * 1024),
        name="last",
    )(*parts)
    return (
        spectra.reshape(here, mem, 2, fields, TRUNC),
        fourier.reshape(here, mem, 2, fields, NLAT),
    )


def solution(mesh):
    in_specs = (
        P("member", None, "lat", None),
        P("member", None, "lat", None),
        P(),
        P(),
        P("lat", "member", None, None, None),
    )
    out_specs = (P("lat", "member", None, None, None), P("lat", "member", None, None, None))
    return jax.shard_map(
        functools.partial(per_device, mesh.shape["lat"], mesh.shape["member"]),
        mesh=mesh, in_specs=in_specs, out_specs=out_specs, check_vma=False,
    )
```

```python
import functools
import math

import jax
import jax.numpy as jnp
from jax import lax
from jax.experimental import pallas as pl
from jax.experimental.pallas import tpu as pltpu
from jax.sharding import PartitionSpec as P

NLAT = 1024
NLON = 2048
TRUNC = 683
NPAD = 768
SPREAD = 2
SG = 8
MESH = pl.DeviceIdType.MESH
F32 = jnp.float32
BF16 = jnp.bfloat16
NT = (((1,), (1,)), ((), ()))
NN = (((1,), (0,)), ((), ()))


def iota(shape, dim):
    return lax.broadcasted_iota(jnp.int32, shape, dim)


def cos_sin(phase, period):
    eighth = period // 8
    quarter = period // 4
    shifted = phase + eighth
    quad = (shifted // quarter) & 3
    x = ((shifted & (quarter - 1)) - eighth).astype(F32) * (2.0 * math.pi / period)
    y = x * x
    s = x * (1.0 + y * (-1.0 / 6 + y * (1.0 / 120 + y * (-1.0 / 5040 + y * (1.0 / 362880)))))
    c = 1.0 + y * (-0.5 + y * (1.0 / 24 + y * (-1.0 / 720 + y * (1.0 / 40320))))
    odd = (quad & 1) == 1
    cos = jnp.where(odd, s, c)
    sin = jnp.where(odd, c, s)
    cos = jnp.where((quad == 1) | (quad == 2), -cos, cos)
    sin = jnp.where(quad >= 2, -sin, sin)
    return cos, sin


def by_parity(x, even_f, odd_f, cols, is_odd):
    even = lax.dot_general(x, even_f[:, cols], NN, preferred_element_type=F32)
    odd = lax.dot_general(x, odd_f[:, cols], NN, preferred_element_type=F32)
    out = []
    for half in range(2):
        lanes = slice(128 * half, 128 * half + 128)
        groups = range(0, x.shape[0], SG)
        out.append([jnp.where(is_odd, odd[i : i + SG, lanes], even[i : i + SG, lanes]) for i in groups])
    return out


def partial_rows(x, even_f, odd_f, wave, acc):
    is_odd = (wave.astype(jnp.int32) & 1) == 1
    for nt in range(NPAD // 256):
        cols = slice(256 * nt, 256 * nt + 256)
        for half, groups in enumerate(by_parity(x, even_f, odd_f, cols, is_odd)):
            start = 256 * nt + 128 * half
            acc[:, start : start + 128] = jnp.concatenate(groups, axis=0)


def forward_rows(x, even_f, odd_f, wave, order, acc, spec):
    w = wave.astype(jnp.int32)
    is_odd = (w & 1) == 1
    for nt in range(NPAD // 256):
        cols = slice(256 * nt, 256 * nt + 256)
        tiles = []
        for half, groups in enumerate(by_parity(x, even_f, odd_f, cols, is_odd)):
            start = 256 * nt + 128 * half
            n = start + iota((SG, 128), 1)
            live = (n >= w) & (w < TRUNC) & (n < TRUNC)
            if acc is not None:
                groups = [g + acc[SG * i : SG * i + SG, start : start + 128] for i, g in enumerate(groups)]
            tiles.append(jnp.concatenate([jnp.where(live, g, 0.0) for g in groups], axis=0))
        value = jnp.concatenate(tiles, axis=1).astype(BF16)
        spec[:, cols] = lax.dot_general(order, value, NN, preferred_element_type=F32).astype(BF16)


def finish_rows(base_of, noise, even_t, odd_t, wave, kids, spec_out, four_out, mf, ready=lambda part: None):
    w = wave.astype(jnp.int32)
    wide = jnp.concatenate([w] * (NPAD // 128), axis=1)
    for s in range(SG):
        rows = slice(s * 2 * mf, (s + 1) * 2 * mf)
        ws = wide[s : s + 1, :TRUNC]
        live = (iota((2 * mf, TRUNC), 1) >= ws) & (ws < TRUNC)
        base = base_of(s).astype(F32)[:, :TRUNC]
        child = (base + jnp.where(live, noise[rows, :].astype(F32), 0.0)).astype(BF16)
        spec_out[rows, :] = child
        kids[rows, :TRUNC] = child
        kids[rows, TRUNC:] = jnp.zeros((2 * mf, NPAD - TRUNC), BF16)
    ready(0)
    for nt in range(NLAT // 256):
        cols = slice(256 * nt, 256 * nt + 256)
        even = lax.dot_general(kids[...], even_t[:, cols], NN, preferred_element_type=F32)
        odd = lax.dot_general(kids[...], odd_t[:, cols], NN, preferred_element_type=F32)
        for s in range(SG):
            rows = slice(s * 2 * mf, (s + 1) * 2 * mf)
            ws = jnp.concatenate([w[s : s + 1, :]] * 2, axis=1)
            is_odd = jnp.broadcast_to((ws & 1) == 1, (2 * mf, 256))
            four_out[rows, cols] = jnp.where(is_odd, odd[rows], even[rows]).astype(BF16)
        ready(nt + 1)


def kernel(
    lat_count, member_count,
    parents_hbm, waves_row_hbm, velocity, tracer, noise,
    spec_v, four_v, acc, last_x, last_noise, last_wave, order, even_t, odd_t, even_l, odd_l,
    parents, waves_row, wave_b, vel, tra, prod, table, four, low, high, sel, recv,
    even_f, odd_f, xmat, spec, kids, noise_v, own_s, low_s, high_s,
    small_sem, ss_sem, sr_sem, in_sem, noise_sem, xs_sem, xr_sem, as_sem, ar_sem,
):
    me = lax.axis_index("lat")
    group = lax.axis_index("member")
    chunks = four.shape[0]
    slots_here = chunks * SG
    halves = 2
    half_count = lat_count // halves
    lat_local = NLAT // lat_count
    mf = vel.shape[0] // lat_local
    chunk_rows = SG * 2 * mf
    fields = mf // 2

    barrier = pltpu.get_barrier_semaphore()
    up = lax.rem(group + 1, member_count)
    down = lax.rem(group + member_count - 1, member_count)

    pieces = 4
    piece = vel.shape[0] // pieces

    def loads(i):
        block = pl.ds(i * piece, piece)
        return (
            pltpu.make_async_copy(velocity.at[block], vel.at[block], in_sem.at[0, i]),
            pltpu.make_async_copy(tracer.at[block], tra.at[block], in_sem.at[1, i]),
        )

    for c in loads(0):
        c.start()

    for o in sorted(range(1, lat_count), key=lambda o: abs(o - lat_count // 2)):
        pl.semaphore_signal(
            barrier, inc=1, device_id={"lat": lax.rem(me + o, lat_count)}, device_id_type=MESH
        )

    pl.semaphore_signal(barrier, inc=1, device_id={"member": up}, device_id_type=MESH)
    pl.semaphore_signal(barrier, inc=1, device_id={"member": down}, device_id_type=MESH)
    load_w = pltpu.make_async_copy(waves_row_hbm, waves_row, small_sem.at[0])
    load_w.start()
    for i in range(1, pieces):
        for c in loads(i):
            c.start()
    load_p = pltpu.make_async_copy(parents_hbm, parents, small_sem.at[1])
    load_p.start()
    load_n = pltpu.make_async_copy(noise, noise_v, noise_sem)
    load_n.start()

    y_count = 128 // lat_local
    z_count = lat_count // y_count
    my_z, my_y = me // y_count, lax.rem(me, y_count)

    def turn_of(k):
        r = z_count - 1 - k
        return (r + 1) // 2 * (1 - 2 * lax.rem(r + 1, 2))

    def target_of(q, i):
        if q < chunks - 1:
            k, y = lax.rem(i, z_count), i // z_count + 1
        else:
            k, y = i // y_count, i + 1
        z = lax.rem(my_z + turn_of(k) + z_count, z_count)
        return z * y_count + lax.rem(my_y + y, y_count)

    def make_table(q, first):
        together = 4

        @pl.loop(0, half_count // together)
        def _(b):
            w = jnp.concatenate(
                [
                    wave_b[
                        pl.ds(pl.multiple_of(target_of(q, first + b * together + j) * slots_here + q * SG, SG), SG), :
                    ]
                    for j in range(together)
                ],
                axis=0,
            ).astype(jnp.int32)
            c, s = cos_sin((w * iota(w.shape, 1)) & (NLON - 1), NLON)
            ct, st = cos_sin((w * 128) & (NLON - 1), NLON)
            weight = jnp.where(w < TRUNC, 1.0 / math.sqrt(NLON), 0.0)
            c = c * weight
            s = -s * weight
            sign = jnp.where((w & 1) == 1, -1.0, 1.0)
            half = NLON // 2
            for t in range(half // 128):
                for factor, offset in ((None, 0), (sign, half)):
                    cc = c if factor is None else c * factor
                    ss = s if factor is None else s * factor
                    for j in range(together):
                        part = slice(j * SG, j * SG + SG)
                        rows = pl.ds(pl.multiple_of((b * together + j) * 2 * SG, 2 * SG), 2 * SG)
                        table[rows, offset + 128 * t : offset + 128 * t + 128] = jnp.concatenate(
                            [cc[part], ss[part]], axis=0
                        ).astype(BF16)
                if t + 1 < half // 128:
                    c, s = c * ct + s * st, s * ct - c * st

    def zonal(q, h):
        first = h * half_count
        make_table(q, first)
        out = lax.dot_general(table[...], prod[...], NT, preferred_element_type=F32)
        four[q, first : first + half_count] = out.astype(BF16).reshape(half_count, 2 * SG, out.shape[1])

    def make_waves():
        load_w.wait()
        for r in range(waves_row.shape[0]):
            row = waves_row[r : r + 1, :].astype(F32)
            wave_b[128 * r : 128 * r + 128, :] = jnp.transpose(jnp.broadcast_to(row, (128, 128)))

    def make_product():
        for i in range(pieces):
            for c in loads(i):
                c.wait()

            @pl.loop(0, piece // 32)
            def _(b):
                rows = pl.ds(pl.multiple_of(i * piece + b * 32, 32), 32)
                prod[rows, :] = (vel[rows, :].astype(F32) * tra[rows, :].astype(F32)).astype(BF16)

    make_waves()
    make_product()

    def x_copies(q, h):
        block = pl.ds(h * half_count, half_count)
        to_up = pltpu.make_async_remote_copy(
            src_ref=four.at[q, block], dst_ref=low.at[q, block],
            send_sem=xs_sem.at[q, h, 0], recv_sem=xr_sem.at[q, h, 0],
            device_id={"member": up}, device_id_type=MESH,
        )
        to_down = pltpu.make_async_remote_copy(
            src_ref=four.at[q, block], dst_ref=high.at[q, block],
            send_sem=xs_sem.at[q, h, 1], recv_sem=xr_sem.at[q, h, 1],
            device_id={"member": down}, device_id_type=MESH,
        )
        return to_up, to_down

    def send_half(q, h, source):
        first = h * half_count
        last = h == halves - 1

        @pl.loop(first, first + half_count - (1 if last else 0))
        def _(i):
            pltpu.make_async_remote_copy(
                src_ref=source.at[q, i], dst_ref=recv.at[q, me],
                send_sem=as_sem.at[q], recv_sem=ar_sem.at[q, my_z],
                device_id={"lat": target_of(q, i)}, device_id_type=MESH,
            ).start()

        if last:
            recv[q, me] = source[q, lat_count - 1]

    zonal(0, 0)
    pl.semaphore_wait(barrier, lat_count + 1)
    send_half(0, 0, four)
    zonal(0, 1)
    send_half(0, 1, four)
    for q in range(1, chunks):
        for h in range(halves):
            zonal(q, h)
            for c in x_copies(q, h):
                c.start()

    def source_of(k):
        return lax.rem(my_z - turn_of(k) + z_count, z_count)

    def make_order():
        row = iota(order.shape, 0)
        col = iota(order.shape, 1)
        slot, member, part, field = row // (2 * mf), row // mf % 2, row // fields % 2, row % fields
        source = ((member * fields + field) * 2 + part) * SG + slot
        order[...] = jnp.where(col == source, 1.0, 0.0).astype(BF16)

    def make_basis(even, odd, rows_are_degrees):
        step = 64
        period = 4 * NLAT
        row_count, lane_count = even.shape
        lanes = lane_count // (2 if rows_are_degrees else 3)
        scale = math.sqrt(2.0 / NLAT)

        @pl.loop(0, lane_count // lanes)
        def _(tile):
            lane = tile * lanes + iota((8, lanes), 1)
            sub = iota((8, lanes), 0)
            turn = 8 * (2 * lane + 1) if rows_are_degrees else 16 * lane
            c8, s8 = cos_sin(turn & (period - 1), period)
            cols = pl.ds(pl.multiple_of(tile * lanes, 128), lanes)

            @pl.loop(0, row_count // step)
            def _(a):
                row = a * step + sub
                if not rows_are_degrees:
                    row = row + (source_of(a // 2) - a // 2) * 128
                phase = row * (2 * lane + 1) if rows_are_degrees else lane * (2 * row + 1)
                c, s = cos_sin(phase & (period - 1), period)
                c = c * scale
                s = s * scale
                for b in range(step // 16):
                    c2, s2 = c * c8 - s * s8, s * c8 + c * s8
                    r16 = pl.ds(pl.multiple_of(a * step + b * 16, 16), 16)
                    even[r16, cols] = jnp.concatenate([c, c2], axis=0).astype(BF16)
                    odd[r16, cols] = jnp.concatenate([s, s2], axis=0).astype(BF16)
                    c, s = c2 * c8 - s2 * s8, s2 * c8 + c2 * s8

    load_p.wait()
    first_member = group * 2
    places = [parents[first_member + m] - first_member + SPREAD for m in range(2)]

    def select_half(q, h):
        width = fields * lat_local

        @pl.loop(h * half_count, (h + 1) * half_count)
        def _(i):
            for m in range(2):
                chosen = None
                for p in range(m, m + 2 * SPREAD + 1):
                    source = (low, four, high)[p // 2]
                    cand = source[q, i, :, (p % 2) * width : (p % 2 + 1) * width]
                    hit = jnp.broadcast_to(places[m] == p, cand.shape)
                    chosen = cand if chosen is None else jnp.where(hit, cand, chosen)
                sel[q, i, :, m * width : (m + 1) * width] = chosen

    def relay(q, h):
        for c in x_copies(q, h):
            c.wait_recv()
        select_half(q, h)
        send_half(q, h, sel)

    relay(1, 0)
    make_basis(even_f, odd_f, False)
    relay(1, 1)
    make_basis(even_t, odd_t, True)
    relay(2, 0)
    make_order()
    relay(2, 1)

    load_n.wait()

    def arrive(q, p, count):
        block = recv.at[q, pl.ds(p * y_count, count)]
        pltpu.make_async_remote_copy(
            src_ref=block, dst_ref=block, send_sem=as_sem.at[q], recv_sem=ar_sem.at[q, p],
            device_id={"lat": me}, device_id_type=MESH,
        ).wait_recv()

    split = z_count - 2

    def shuffle(q, begin, end):
        per = 128 // lat_local
        lane = iota((2 * SG, 128), 1) // lat_local
        low_half = lane < 2
        even_block = (lane & 1) == 0

        def swap(x, y, mask, width):
            left = jnp.where(mask, x, pltpu.roll(y, width, 1))
            right = jnp.where(mask, pltpu.roll(x, 128 - width, 1), y)
            return left, right

        def arrange(p, k):
            target = pl.ds(pl.multiple_of(k * 128, 128), 128)
            for t in range(mf // per):
                x0, x1, x2, x3 = [recv[q, p * per + i, :, 128 * t : 128 * t + 128] for i in range(per)]
                x0, x2 = swap(x0, x2, low_half, 2 * lat_local)
                x1, x3 = swap(x1, x3, low_half, 2 * lat_local)
                x0, x1 = swap(x0, x1, even_block, lat_local)
                x2, x3 = swap(x2, x3, even_block, lat_local)
                for j, x in enumerate((x0, x1, x2, x3)):
                    xmat[(t * per + j) * 2 * SG : (t * per + j + 1) * 2 * SG, target] = x

        @pl.loop(begin, min(end, z_count - 1))
        def _(k):
            p = source_of(k)
            arrive(q, p, per)
            arrange(p, k)

        if end == z_count:
            arrive(q, my_z, per - 1)
            arrange(my_z, z_count - 1)

    def forward(q):
        shuffle(q, 0, z_count)
        product(q)

    def own_wave(q):
        return wave_b[pl.ds(pl.multiple_of(me * slots_here + q * SG, SG), SG), :]

    def product(q):
        forward_rows(xmat[...], even_f, odd_f, own_wave(q), order[...], None, spec)

    def finish(q, base_of):
        block = pl.ds(q * chunk_rows, chunk_rows)
        finish_rows(
            base_of, noise_v.at[block], even_t, odd_t, own_wave(q), kids,
            spec_v.at[block], four_v.at[block], mf,
        )

    def own_of(s):
        return spec[s * 2 * mf : (s + 1) * 2 * mf, :]

    def s_copies():
        to_up = pltpu.make_async_remote_copy(
            src_ref=own_s, dst_ref=low_s, send_sem=ss_sem.at[0], recv_sem=sr_sem.at[0],
            device_id={"member": up}, device_id_type=MESH,
        )
        to_down = pltpu.make_async_remote_copy(
            src_ref=own_s, dst_ref=high_s, send_sem=ss_sem.at[1], recv_sem=sr_sem.at[1],
            device_id={"member": down}, device_id_type=MESH,
        )
        return to_up, to_down

    def share():
        for s in range(SG):
            own_s[s * 2 * mf : (s + 1) * 2 * mf, :] = own_of(s)
        for c in s_copies():
            c.start()

    def chosen_of(s):
        out = []
        for m in range(2):
            chosen = None
            for p in range(m, m + 2 * SPREAD + 1):
                source = (low_s, own_s, high_s)[p // 2]
                start = s * 2 * mf + (p % 2) * mf
                cand = source[start : start + mf, :]
                hit = jnp.broadcast_to(places[m] == p, cand.shape)
                chosen = cand if chosen is None else jnp.where(hit, cand, chosen)
            out.append(chosen)
        return jnp.concatenate(out, axis=0)

    forward(0)
    share()
    forward(1)
    finish(1, own_of)
    for c in s_copies():
        c.wait_recv()
    finish(0, chosen_of)
    last_noise[...] = noise_v[2 * chunk_rows : 3 * chunk_rows, :]
    last_wave[...] = own_wave(2)
    even_l[...] = even_f[split * 128 :, :]
    odd_l[...] = odd_f[split * 128 :, :]
    shuffle(2, 0, split)
    early = pl.ds(0, split * 128)
    partial_rows(xmat[:, :split * 128], even_f.at[early], odd_f.at[early], own_wave(2), acc)
    shuffle(2, split, z_count)
    last_x[...] = xmat[:, split * 128 :]

    for c in s_copies():
        c.wait_send()
    for q in range(chunks):
        if q > 0:
            for h in range(halves):
                for c in x_copies(q, h):
                    c.wait_send()
        pltpu.make_async_remote_copy(
            src_ref=sel.at[q, pl.ds(0, lat_count - 1)], dst_ref=recv.at[q, pl.ds(0, lat_count - 1)],
            send_sem=as_sem.at[q], recv_sem=ar_sem.at[q, 0], device_id={"lat": me}, device_id_type=MESH,
        ).wait_send()


def tail(
    mf, spec_v, four_v, acc, x, noise, wave, order, even_t, odd_t, even_l, odd_l,
    spectra_out, fourier_out, spec, kids, spec_l, four_l, sem,
):
    done = spec_v.shape[0]
    rows = x.shape[0]
    copies = [
        pltpu.make_async_copy(spec_v, spectra_out.at[pl.ds(0, done)], sem.at[0]),
        pltpu.make_async_copy(four_v, fourier_out.at[pl.ds(0, done)], sem.at[1]),
    ]
    for c in copies:
        c.start()
    w = wave[...]
    forward_rows(x[...], even_l, odd_l, w, order[...], acc, spec)

    def ready(part):
        if part == 0:
            c = pltpu.make_async_copy(spec_l, spectra_out.at[pl.ds(done, rows)], sem.at[2])
        else:
            cols = pl.ds(256 * (part - 1), 256)
            c = pltpu.make_async_copy(four_l.at[:, cols], fourier_out.at[pl.ds(done, rows), cols], sem.at[2 + part])
        copies.append(c)
        c.start()

    finish_rows(
        lambda s: spec[s * 2 * mf : (s + 1) * 2 * mf, :], noise, even_t, odd_t, w, kids, spec_l, four_l, mf, ready
    )
    for c in copies:
        c.wait()


def per_device(lat_count, member_count, velocity, tracer, wave_slots, parents, noise):
    mem, fields, lat_local, lon = velocity.shape
    slots = wave_slots.shape[0]
    here = slots // lat_count
    chunks = here // SG
    rows = mem * fields * lat_local
    mf = mem * fields
    out_rows = here * mem * 2 * fields
    chunk_rows = SG * 2 * mf
    msg = (chunks, lat_count, 2 * SG, rows)
    dma = pltpu.SemaphoreType.DMA
    hbm = pl.BlockSpec(memory_space=pltpu.HBM)
    vmem = pl.BlockSpec(memory_space=pltpu.VMEM)
    early = out_rows - chunk_rows
    middle = (
        jax.ShapeDtypeStruct((early, TRUNC), BF16),
        jax.ShapeDtypeStruct((early, NLAT), BF16),
        jax.ShapeDtypeStruct((chunk_rows, NPAD), F32),
        jax.ShapeDtypeStruct((chunk_rows, 256), BF16),
        jax.ShapeDtypeStruct((chunk_rows, TRUNC), BF16),
        jax.ShapeDtypeStruct((SG, 128), F32),
        jax.ShapeDtypeStruct((chunk_rows, chunk_rows), BF16),
        jax.ShapeDtypeStruct((NPAD, NLAT), BF16),
        jax.ShapeDtypeStruct((NPAD, NLAT), BF16),
        jax.ShapeDtypeStruct((256, NPAD), BF16),
        jax.ShapeDtypeStruct((256, NPAD), BF16),
    )
    parts = pl.pallas_call(
        functools.partial(kernel, lat_count, member_count),
        out_shape=middle,
        in_specs=[hbm] * 5,
        out_specs=(vmem,) * len(middle),
        scratch_shapes=[
            pltpu.SMEM(parents.shape, jnp.int32),
            pltpu.VMEM((slots // 128, 128), jnp.int32),
            pltpu.VMEM((slots, 128), F32),
            pltpu.VMEM((rows, lon), BF16),
            pltpu.VMEM((rows, lon), BF16),
            pltpu.VMEM((rows, lon), BF16),
            pltpu.VMEM((lat_count // 2 * 2 * SG, lon), BF16),
            pltpu.VMEM(msg, BF16),
            pltpu.VMEM(msg, BF16),
            pltpu.VMEM(msg, BF16),
            pltpu.VMEM(msg, BF16),
            pltpu.VMEM(msg, BF16),
            pltpu.VMEM((NLAT, NPAD), BF16),
            pltpu.VMEM((NLAT, NPAD), BF16),
            pltpu.VMEM((chunk_rows, NLAT), BF16),
            pltpu.VMEM((chunk_rows, NPAD), BF16),
            pltpu.VMEM((chunk_rows, NPAD), BF16),
            pltpu.VMEM((out_rows, TRUNC), BF16),
            pltpu.VMEM((chunk_rows, NPAD), BF16),
            pltpu.VMEM((chunk_rows, NPAD), BF16),
            pltpu.VMEM((chunk_rows, NPAD), BF16),
            dma((2,)),
            dma((2,)),
            dma((2,)),
            dma((2, 4)),
            dma,
            dma((chunks, 2, 2)),
            dma((chunks, 2, 2)),
            dma((chunks,)),
            dma((chunks, lat_count * lat_local // 128)),
        ],
        compiler_params=pltpu.CompilerParams(
            collective_id=0, has_side_effects=True, vmem_limit_bytes=44 * 1024 * 1024
        ),
        name="transform",
    )(
        pltpu.with_memory_space_constraint(parents, pltpu.HBM),
        pltpu.with_memory_space_constraint(wave_slots.reshape(slots // 128, 128), pltpu.HBM),
        pltpu.with_memory_space_constraint(velocity.reshape(rows, lon), pltpu.HBM),
        pltpu.with_memory_space_constraint(tracer.reshape(rows, lon), pltpu.HBM),
        pltpu.with_memory_space_constraint(noise.reshape(out_rows, TRUNC), pltpu.HBM),
    )
    spectra, fourier = pl.pallas_call(
        functools.partial(tail, mf),
        out_shape=(
            jax.ShapeDtypeStruct((out_rows, TRUNC), BF16),
            jax.ShapeDtypeStruct((out_rows, NLAT), BF16),
        ),
        in_specs=[vmem] * len(middle),
        out_specs=(hbm, hbm),
        scratch_shapes=[
            pltpu.VMEM((chunk_rows, NPAD), BF16),
            pltpu.VMEM((chunk_rows, NPAD), BF16),
            pltpu.VMEM((chunk_rows, TRUNC), BF16),
            pltpu.VMEM((chunk_rows, NLAT), BF16),
            dma((3 + NLAT // 256,)),
        ],
        compiler_params=pltpu.CompilerParams(vmem_limit_bytes=44 * 1024 * 1024),
        name="last",
    )(*parts)
    return (
        spectra.reshape(here, mem, 2, fields, TRUNC),
        fourier.reshape(here, mem, 2, fields, NLAT),
    )


def solution(mesh):
    in_specs = (
        P("member", None, "lat", None),
        P("member", None, "lat", None),
        P(),
        P(),
        P("lat", "member", None, None, None),
    )
    out_specs = (P("lat", "member", None, None, None), P("lat", "member", None, None, None))
    return jax.shard_map(
        functools.partial(per_device, mesh.shape["lat"], mesh.shape["member"]),
        mesh=mesh, in_specs=in_specs, out_specs=out_specs, check_vma=False,
    )
```

```python
import functools
import math

import jax
import jax.numpy as jnp
from jax import lax
from jax.experimental import pallas as pl
from jax.experimental.pallas import tpu as pltpu
from jax.sharding import PartitionSpec as P

NLAT = 1024
NLON = 2048
TRUNC = 683
NPAD = 768
SPREAD = 2
SG = 8
MESH = pl.DeviceIdType.MESH
F32 = jnp.float32
BF16 = jnp.bfloat16
NT = (((1,), (1,)), ((), ()))
NN = (((1,), (0,)), ((), ()))


def iota(shape, dim):
    return lax.broadcasted_iota(jnp.int32, shape, dim)


def cos_sin(phase, period):
    eighth = period // 8
    quarter = period // 4
    shifted = phase + eighth
    quad = (shifted // quarter) & 3
    x = ((shifted & (quarter - 1)) - eighth).astype(F32) * (2.0 * math.pi / period)
    y = x * x
    s = x * (1.0 + y * (-1.0 / 6 + y * (1.0 / 120 + y * (-1.0 / 5040 + y * (1.0 / 362880)))))
    c = 1.0 + y * (-0.5 + y * (1.0 / 24 + y * (-1.0 / 720 + y * (1.0 / 40320))))
    odd = (quad & 1) == 1
    cos = jnp.where(odd, s, c)
    sin = jnp.where(odd, c, s)
    cos = jnp.where((quad == 1) | (quad == 2), -cos, cos)
    sin = jnp.where(quad >= 2, -sin, sin)
    return cos, sin


def by_parity(x, even_f, odd_f, cols, is_odd):
    even = lax.dot_general(x, even_f[:, cols], NN, preferred_element_type=F32)
    odd = lax.dot_general(x, odd_f[:, cols], NN, preferred_element_type=F32)
    out = []
    for half in range(2):
        lanes = slice(128 * half, 128 * half + 128)
        groups = range(0, x.shape[0], SG)
        out.append([jnp.where(is_odd, odd[i : i + SG, lanes], even[i : i + SG, lanes]) for i in groups])
    return out


def partial_rows(x, even_f, odd_f, wave, acc):
    is_odd = (wave.astype(jnp.int32) & 1) == 1
    for nt in range(NPAD // 256):
        cols = slice(256 * nt, 256 * nt + 256)
        for half, groups in enumerate(by_parity(x, even_f, odd_f, cols, is_odd)):
            start = 256 * nt + 128 * half
            acc[:, start : start + 128] = jnp.concatenate(groups, axis=0)


def forward_rows(x, even_f, odd_f, wave, order, acc, spec):
    w = wave.astype(jnp.int32)
    is_odd = (w & 1) == 1
    for nt in range(NPAD // 256):
        cols = slice(256 * nt, 256 * nt + 256)
        tiles = []
        for half, groups in enumerate(by_parity(x, even_f, odd_f, cols, is_odd)):
            start = 256 * nt + 128 * half
            n = start + iota((SG, 128), 1)
            live = (n >= w) & (w < TRUNC) & (n < TRUNC)
            if acc is not None:
                groups = [g + acc[SG * i : SG * i + SG, start : start + 128] for i, g in enumerate(groups)]
            tiles.append(jnp.concatenate([jnp.where(live, g, 0.0) for g in groups], axis=0))
        value = jnp.concatenate(tiles, axis=1).astype(BF16)
        spec[:, cols] = lax.dot_general(order, value, NN, preferred_element_type=F32).astype(BF16)


def finish_rows(base_of, noise, even_t, odd_t, wave, kids, spec_out, four_out, mf, ready=lambda part: None):
    w = wave.astype(jnp.int32)
    wide = jnp.concatenate([w] * (NPAD // 128), axis=1)
    for s in range(SG):
        rows = slice(s * 2 * mf, (s + 1) * 2 * mf)
        ws = wide[s : s + 1, :TRUNC]
        live = (iota((2 * mf, TRUNC), 1) >= ws) & (ws < TRUNC)
        base = base_of(s).astype(F32)[:, :TRUNC]
        child = (base + jnp.where(live, noise[rows, :].astype(F32), 0.0)).astype(BF16)
        spec_out[rows, :] = child
        kids[rows, :TRUNC] = child
        kids[rows, TRUNC:] = jnp.zeros((2 * mf, NPAD - TRUNC), BF16)
    ready(0)
    for nt in range(NLAT // 256):
        cols = slice(256 * nt, 256 * nt + 256)
        even = lax.dot_general(kids[...], even_t[:, cols], NN, preferred_element_type=F32)
        odd = lax.dot_general(kids[...], odd_t[:, cols], NN, preferred_element_type=F32)
        for s in range(SG):
            rows = slice(s * 2 * mf, (s + 1) * 2 * mf)
            ws = jnp.concatenate([w[s : s + 1, :]] * 2, axis=1)
            is_odd = jnp.broadcast_to((ws & 1) == 1, (2 * mf, 256))
            four_out[rows, cols] = jnp.where(is_odd, odd[rows], even[rows]).astype(BF16)
        ready(nt + 1)


def kernel(
    lat_count, member_count,
    parents_hbm, waves_row_hbm, velocity, tracer, noise,
    spec_v, four_v, acc, last_x, last_noise, last_wave, order, even_t, odd_t, even_l, odd_l,
    parents, waves_row, wave_b, vel, tra, prod, table, four, low, high, sel, recv,
    even_f, odd_f, xmat, spec, kids, noise_v, own_s, low_s, high_s,
    small_sem, ss_sem, sr_sem, in_sem, noise_sem, xs_sem, xr_sem, as_sem, ar_sem,
):
    me = lax.axis_index("lat")
    group = lax.axis_index("member")
    chunks = four.shape[0]
    slots_here = chunks * SG
    halves = 2
    half_count = lat_count // halves
    lat_local = NLAT // lat_count
    mf = vel.shape[0] // lat_local
    chunk_rows = SG * 2 * mf
    fields = mf // 2

    barrier = pltpu.get_barrier_semaphore()
    up = lax.rem(group + 1, member_count)
    down = lax.rem(group + member_count - 1, member_count)

    pieces = 4
    piece = vel.shape[0] // pieces

    def loads(i):
        block = pl.ds(i * piece, piece)
        return (
            pltpu.make_async_copy(velocity.at[block], vel.at[block], in_sem.at[0, i]),
            pltpu.make_async_copy(tracer.at[block], tra.at[block], in_sem.at[1, i]),
        )

    for c in loads(0):
        c.start()

    for o in sorted(range(1, lat_count), key=lambda o: abs(o - lat_count // 2)):
        pl.semaphore_signal(
            barrier, inc=1, device_id={"lat": lax.rem(me + o, lat_count)}, device_id_type=MESH
        )

    pl.semaphore_signal(barrier, inc=1, device_id={"member": up}, device_id_type=MESH)
    pl.semaphore_signal(barrier, inc=1, device_id={"member": down}, device_id_type=MESH)
    load_w = pltpu.make_async_copy(waves_row_hbm, waves_row, small_sem.at[0])
    load_w.start()
    for i in range(1, pieces):
        for c in loads(i):
            c.start()
    load_p = pltpu.make_async_copy(parents_hbm, parents, small_sem.at[1])
    load_p.start()
    load_n = pltpu.make_async_copy(noise, noise_v, noise_sem)
    load_n.start()

    y_count = 128 // lat_local
    z_count = lat_count // y_count
    my_z, my_y = me // y_count, lax.rem(me, y_count)

    def turn_of(k):
        r = z_count - 1 - k
        return (r + 1) // 2 * (1 - 2 * lax.rem(r + 1, 2))

    def target_of(q, i):
        if q < chunks - 1:
            k, y = lax.rem(i, z_count), i // z_count + 1
        else:
            k, y = i // y_count, i + 1
        z = lax.rem(my_z + turn_of(k) + z_count, z_count)
        return z * y_count + lax.rem(my_y + y, y_count)

    def make_table(q, first):
        together = 4

        @pl.loop(0, half_count // together)
        def _(b):
            w = jnp.concatenate(
                [
                    wave_b[
                        pl.ds(pl.multiple_of(target_of(q, first + b * together + j) * slots_here + q * SG, SG), SG), :
                    ]
                    for j in range(together)
                ],
                axis=0,
            ).astype(jnp.int32)
            c, s = cos_sin((w * iota(w.shape, 1)) & (NLON - 1), NLON)
            ct, st = cos_sin((w * 128) & (NLON - 1), NLON)
            weight = jnp.where(w < TRUNC, 1.0 / math.sqrt(NLON), 0.0)
            c = c * weight
            s = -s * weight
            sign = jnp.where((w & 1) == 1, -1.0, 1.0)
            half = NLON // 2
            for t in range(half // 128):
                for factor, offset in ((None, 0), (sign, half)):
                    cc = c if factor is None else c * factor
                    ss = s if factor is None else s * factor
                    for j in range(together):
                        part = slice(j * SG, j * SG + SG)
                        rows = pl.ds(pl.multiple_of((b * together + j) * 2 * SG, 2 * SG), 2 * SG)
                        table[rows, offset + 128 * t : offset + 128 * t + 128] = jnp.concatenate(
                            [cc[part], ss[part]], axis=0
                        ).astype(BF16)
                if t + 1 < half // 128:
                    c, s = c * ct + s * st, s * ct - c * st

    def zonal(q, h):
        first = h * half_count
        make_table(q, first)
        out = lax.dot_general(table[...], prod[...], NT, preferred_element_type=F32)
        four[q, first : first + half_count] = out.astype(BF16).reshape(half_count, 2 * SG, out.shape[1])

    def make_waves():
        load_w.wait()
        for r in range(waves_row.shape[0]):
            row = waves_row[r : r + 1, :].astype(F32)
            wave_b[128 * r : 128 * r + 128, :] = jnp.transpose(jnp.broadcast_to(row, (128, 128)))

    def make_product():
        for i in range(pieces):
            for c in loads(i):
                c.wait()

            @pl.loop(0, piece // 32)
            def _(b):
                rows = pl.ds(pl.multiple_of(i * piece + b * 32, 32), 32)
                prod[rows, :] = (vel[rows, :].astype(F32) * tra[rows, :].astype(F32)).astype(BF16)

    make_waves()
    make_product()

    def x_copies(q, h):
        block = pl.ds(h * half_count, half_count)
        to_up = pltpu.make_async_remote_copy(
            src_ref=four.at[q, block], dst_ref=low.at[q, block],
            send_sem=xs_sem.at[q, h, 0], recv_sem=xr_sem.at[q, h, 0],
            device_id={"member": up}, device_id_type=MESH,
        )
        to_down = pltpu.make_async_remote_copy(
            src_ref=four.at[q, block], dst_ref=high.at[q, block],
            send_sem=xs_sem.at[q, h, 1], recv_sem=xr_sem.at[q, h, 1],
            device_id={"member": down}, device_id_type=MESH,
        )
        return to_up, to_down

    def send_half(q, h, source):
        first = h * half_count
        last = h == halves - 1

        @pl.loop(first, first + half_count - (1 if last else 0))
        def _(i):
            pltpu.make_async_remote_copy(
                src_ref=source.at[q, i], dst_ref=recv.at[q, me],
                send_sem=as_sem.at[q], recv_sem=ar_sem.at[q, my_z],
                device_id={"lat": target_of(q, i)}, device_id_type=MESH,
            ).start()

        if last:
            recv[q, me] = source[q, lat_count - 1]

    zonal(0, 0)
    pl.semaphore_wait(barrier, lat_count + 1)
    send_half(0, 0, four)
    def coefficients(q, h):
        zonal(q, h)
        for c in x_copies(q, h):
            c.start()

    coefficients(1, 0)
    zonal(0, 1)
    send_half(0, 1, four)
    coefficients(1, 1)
    for q in range(2, chunks):
        for h in range(halves):
            coefficients(q, h)

    def source_of(k):
        return lax.rem(my_z - turn_of(k) + z_count, z_count)

    def make_order():
        row = iota(order.shape, 0)
        col = iota(order.shape, 1)
        slot, member, part, field = row // (2 * mf), row // mf % 2, row // fields % 2, row % fields
        source = ((member * fields + field) * 2 + part) * SG + slot
        order[...] = jnp.where(col == source, 1.0, 0.0).astype(BF16)

    def make_basis(even, odd, rows_are_degrees):
        step = 64
        period = 4 * NLAT
        row_count, lane_count = even.shape
        lanes = lane_count // (2 if rows_are_degrees else 3)
        scale = math.sqrt(2.0 / NLAT)

        @pl.loop(0, lane_count // lanes)
        def _(tile):
            lane = tile * lanes + iota((8, lanes), 1)
            sub = iota((8, lanes), 0)
            turn = 8 * (2 * lane + 1) if rows_are_degrees else 16 * lane
            c8, s8 = cos_sin(turn & (period - 1), period)
            cols = pl.ds(pl.multiple_of(tile * lanes, 128), lanes)

            @pl.loop(0, row_count // step)
            def _(a):
                row = a * step + sub
                if not rows_are_degrees:
                    row = row + (source_of(a // 2) - a // 2) * 128
                phase = row * (2 * lane + 1) if rows_are_degrees else lane * (2 * row + 1)
                c, s = cos_sin(phase & (period - 1), period)
                c = c * scale
                s = s * scale
                for b in range(step // 16):
                    c2, s2 = c * c8 - s * s8, s * c8 + c * s8
                    r16 = pl.ds(pl.multiple_of(a * step + b * 16, 16), 16)
                    even[r16, cols] = jnp.concatenate([c, c2], axis=0).astype(BF16)
                    odd[r16, cols] = jnp.concatenate([s, s2], axis=0).astype(BF16)
                    c, s = c2 * c8 - s2 * s8, s2 * c8 + c2 * s8

    load_p.wait()
    first_member = group * 2
    places = [parents[first_member + m] - first_member + SPREAD for m in range(2)]

    def select_half(q, h):
        width = fields * lat_local

        @pl.loop(h * half_count, (h + 1) * half_count)
        def _(i):
            for m in range(2):
                chosen = None
                for p in range(m, m + 2 * SPREAD + 1):
                    source = (low, four, high)[p // 2]
                    cand = source[q, i, :, (p % 2) * width : (p % 2 + 1) * width]
                    hit = jnp.broadcast_to(places[m] == p, cand.shape)
                    chosen = cand if chosen is None else jnp.where(hit, cand, chosen)
                sel[q, i, :, m * width : (m + 1) * width] = chosen

    def relay(q, h):
        for c in x_copies(q, h):
            c.wait_recv()
        select_half(q, h)
        send_half(q, h, sel)

    relay(1, 0)
    relay(1, 1)
    make_basis(even_f, odd_f, False)
    relay(2, 0)
    make_order()
    relay(2, 1)
    make_basis(even_t, odd_t, True)

    load_n.wait()

    def arrive(q, p, count):
        block = recv.at[q, pl.ds(p * y_count, count)]
        pltpu.make_async_remote_copy(
            src_ref=block, dst_ref=block, send_sem=as_sem.at[q], recv_sem=ar_sem.at[q, p],
            device_id={"lat": me}, device_id_type=MESH,
        ).wait_recv()

    split = z_count - 2

    def shuffle(q, begin, end, out=xmat, shift=0):
        per = 128 // lat_local
        lane = iota((2 * SG, 128), 1) // lat_local
        low_half = lane < 2
        even_block = (lane & 1) == 0

        def swap(x, y, mask, width):
            left = jnp.where(mask, x, pltpu.roll(y, width, 1))
            right = jnp.where(mask, pltpu.roll(x, 128 - width, 1), y)
            return left, right

        def arrange(p, k):
            target = pl.ds(pl.multiple_of((k - shift) * 128, 128), 128)
            for t in range(mf // per):
                x0, x1, x2, x3 = [recv[q, p * per + i, :, 128 * t : 128 * t + 128] for i in range(per)]
                x0, x2 = swap(x0, x2, low_half, 2 * lat_local)
                x1, x3 = swap(x1, x3, low_half, 2 * lat_local)
                x0, x1 = swap(x0, x1, even_block, lat_local)
                x2, x3 = swap(x2, x3, even_block, lat_local)
                for j, x in enumerate((x0, x1, x2, x3)):
                    out[(t * per + j) * 2 * SG : (t * per + j + 1) * 2 * SG, target] = x

        @pl.loop(begin, min(end, z_count - 1))
        def _(k):
            p = source_of(k)
            arrive(q, p, per)
            arrange(p, k)

        if end == z_count:
            arrive(q, my_z, per - 1)
            arrange(my_z, z_count - 1)

    def forward(q):
        shuffle(q, 0, z_count)
        product(q)

    def own_wave(q):
        return wave_b[pl.ds(pl.multiple_of(me * slots_here + q * SG, SG), SG), :]

    def product(q):
        forward_rows(xmat[...], even_f, odd_f, own_wave(q), order[...], None, spec)

    def finish(q, base_of):
        block = pl.ds(q * chunk_rows, chunk_rows)
        finish_rows(
            base_of, noise_v.at[block], even_t, odd_t, own_wave(q), kids,
            spec_v.at[block], four_v.at[block], mf,
        )

    def own_of(s):
        return spec[s * 2 * mf : (s + 1) * 2 * mf, :]

    def s_copies():
        to_up = pltpu.make_async_remote_copy(
            src_ref=own_s, dst_ref=low_s, send_sem=ss_sem.at[0], recv_sem=sr_sem.at[0],
            device_id={"member": up}, device_id_type=MESH,
        )
        to_down = pltpu.make_async_remote_copy(
            src_ref=own_s, dst_ref=high_s, send_sem=ss_sem.at[1], recv_sem=sr_sem.at[1],
            device_id={"member": down}, device_id_type=MESH,
        )
        return to_up, to_down

    def share():
        for s in range(SG):
            own_s[s * 2 * mf : (s + 1) * 2 * mf, :] = own_of(s)
        for c in s_copies():
            c.start()

    def chosen_of(s):
        out = []
        for m in range(2):
            chosen = None
            for p in range(m, m + 2 * SPREAD + 1):
                source = (low_s, own_s, high_s)[p // 2]
                start = s * 2 * mf + (p % 2) * mf
                cand = source[start : start + mf, :]
                hit = jnp.broadcast_to(places[m] == p, cand.shape)
                chosen = cand if chosen is None else jnp.where(hit, cand, chosen)
            out.append(chosen)
        return jnp.concatenate(out, axis=0)

    forward(0)
    share()
    forward(1)
    finish(1, own_of)
    for c in s_copies():
        c.wait_recv()
    finish(0, chosen_of)
    last_noise[...] = noise_v[2 * chunk_rows : 3 * chunk_rows, :]
    last_wave[...] = own_wave(2)
    even_l[...] = even_f[split * 128 :, :]
    odd_l[...] = odd_f[split * 128 :, :]
    shuffle(2, 0, split)
    early = pl.ds(0, split * 128)
    partial_rows(xmat[:, :split * 128], even_f.at[early], odd_f.at[early], own_wave(2), acc)
    shuffle(2, split, z_count, last_x, split)

    for c in s_copies():
        c.wait_send()
    for q in range(chunks):
        if q > 0:
            for h in range(halves):
                for c in x_copies(q, h):
                    c.wait_send()
        pltpu.make_async_remote_copy(
            src_ref=sel.at[q, pl.ds(0, lat_count - 1)], dst_ref=recv.at[q, pl.ds(0, lat_count - 1)],
            send_sem=as_sem.at[q], recv_sem=ar_sem.at[q, 0], device_id={"lat": me}, device_id_type=MESH,
        ).wait_send()


def tail(
    mf, spec_v, four_v, acc, x, noise, wave, order, even_t, odd_t, even_l, odd_l,
    spectra_out, fourier_out, spec, kids, spec_l, four_l, sem,
):
    done = spec_v.shape[0]
    rows = x.shape[0]
    copies = [
        pltpu.make_async_copy(spec_v, spectra_out.at[pl.ds(0, done)], sem.at[0]),
        pltpu.make_async_copy(four_v, fourier_out.at[pl.ds(0, done)], sem.at[1]),
    ]
    for c in copies:
        c.start()
    w = wave[...]
    forward_rows(x[...], even_l, odd_l, w, order[...], acc, spec)

    def ready(part):
        if part == 0:
            c = pltpu.make_async_copy(spec_l, spectra_out.at[pl.ds(done, rows)], sem.at[2])
        else:
            cols = pl.ds(256 * (part - 1), 256)
            c = pltpu.make_async_copy(four_l.at[:, cols], fourier_out.at[pl.ds(done, rows), cols], sem.at[2 + part])
        copies.append(c)
        c.start()

    finish_rows(
        lambda s: spec[s * 2 * mf : (s + 1) * 2 * mf, :], noise, even_t, odd_t, w, kids, spec_l, four_l, mf, ready
    )
    for c in copies:
        c.wait()


def per_device(lat_count, member_count, velocity, tracer, wave_slots, parents, noise):
    mem, fields, lat_local, lon = velocity.shape
    slots = wave_slots.shape[0]
    here = slots // lat_count
    chunks = here // SG
    rows = mem * fields * lat_local
    mf = mem * fields
    out_rows = here * mem * 2 * fields
    chunk_rows = SG * 2 * mf
    msg = (chunks, lat_count, 2 * SG, rows)
    dma = pltpu.SemaphoreType.DMA
    hbm = pl.BlockSpec(memory_space=pltpu.HBM)
    vmem = pl.BlockSpec(memory_space=pltpu.VMEM)
    early = out_rows - chunk_rows
    middle = (
        jax.ShapeDtypeStruct((early, TRUNC), BF16),
        jax.ShapeDtypeStruct((early, NLAT), BF16),
        jax.ShapeDtypeStruct((chunk_rows, NPAD), F32),
        jax.ShapeDtypeStruct((chunk_rows, 256), BF16),
        jax.ShapeDtypeStruct((chunk_rows, TRUNC), BF16),
        jax.ShapeDtypeStruct((SG, 128), F32),
        jax.ShapeDtypeStruct((chunk_rows, chunk_rows), BF16),
        jax.ShapeDtypeStruct((NPAD, NLAT), BF16),
        jax.ShapeDtypeStruct((NPAD, NLAT), BF16),
        jax.ShapeDtypeStruct((256, NPAD), BF16),
        jax.ShapeDtypeStruct((256, NPAD), BF16),
    )
    parts = pl.pallas_call(
        functools.partial(kernel, lat_count, member_count),
        out_shape=middle,
        in_specs=[hbm] * 5,
        out_specs=(vmem,) * len(middle),
        scratch_shapes=[
            pltpu.SMEM(parents.shape, jnp.int32),
            pltpu.VMEM((slots // 128, 128), jnp.int32),
            pltpu.VMEM((slots, 128), F32),
            pltpu.VMEM((rows, lon), BF16),
            pltpu.VMEM((rows, lon), BF16),
            pltpu.VMEM((rows, lon), BF16),
            pltpu.VMEM((lat_count // 2 * 2 * SG, lon), BF16),
            pltpu.VMEM(msg, BF16),
            pltpu.VMEM(msg, BF16),
            pltpu.VMEM(msg, BF16),
            pltpu.VMEM(msg, BF16),
            pltpu.VMEM(msg, BF16),
            pltpu.VMEM((NLAT, NPAD), BF16),
            pltpu.VMEM((NLAT, NPAD), BF16),
            pltpu.VMEM((chunk_rows, NLAT), BF16),
            pltpu.VMEM((chunk_rows, NPAD), BF16),
            pltpu.VMEM((chunk_rows, NPAD), BF16),
            pltpu.VMEM((out_rows, TRUNC), BF16),
            pltpu.VMEM((chunk_rows, NPAD), BF16),
            pltpu.VMEM((chunk_rows, NPAD), BF16),
            pltpu.VMEM((chunk_rows, NPAD), BF16),
            dma((2,)),
            dma((2,)),
            dma((2,)),
            dma((2, 4)),
            dma,
            dma((chunks, 2, 2)),
            dma((chunks, 2, 2)),
            dma((chunks,)),
            dma((chunks, lat_count * lat_local // 128)),
        ],
        compiler_params=pltpu.CompilerParams(
            collective_id=0, has_side_effects=True, vmem_limit_bytes=44 * 1024 * 1024
        ),
        name="transform",
    )(
        pltpu.with_memory_space_constraint(parents, pltpu.HBM),
        pltpu.with_memory_space_constraint(wave_slots.reshape(slots // 128, 128), pltpu.HBM),
        pltpu.with_memory_space_constraint(velocity.reshape(rows, lon), pltpu.HBM),
        pltpu.with_memory_space_constraint(tracer.reshape(rows, lon), pltpu.HBM),
        pltpu.with_memory_space_constraint(noise.reshape(out_rows, TRUNC), pltpu.HBM),
    )
    spectra, fourier = pl.pallas_call(
        functools.partial(tail, mf),
        out_shape=(
            jax.ShapeDtypeStruct((out_rows, TRUNC), BF16),
            jax.ShapeDtypeStruct((out_rows, NLAT), BF16),
        ),
        in_specs=[vmem] * len(middle),
        out_specs=(hbm, hbm),
        scratch_shapes=[
            pltpu.VMEM((chunk_rows, NPAD), BF16),
            pltpu.VMEM((chunk_rows, NPAD), BF16),
            pltpu.VMEM((chunk_rows, TRUNC), BF16),
            pltpu.VMEM((chunk_rows, NLAT), BF16),
            dma((3 + NLAT // 256,)),
        ],
        compiler_params=pltpu.CompilerParams(vmem_limit_bytes=44 * 1024 * 1024),
        name="last",
    )(*parts)
    return (
        spectra.reshape(here, mem, 2, fields, TRUNC),
        fourier.reshape(here, mem, 2, fields, NLAT),
    )


def solution(mesh):
    in_specs = (
        P("member", None, "lat", None),
        P("member", None, "lat", None),
        P(),
        P(),
        P("lat", "member", None, None, None),
    )
    out_specs = (P("lat", "member", None, None, None), P("lat", "member", None, None, None))
    return jax.shard_map(
        functools.partial(per_device, mesh.shape["lat"], mesh.shape["member"]),
        mesh=mesh, in_specs=in_specs, out_specs=out_specs, check_vma=False,
    )
```
